32 devices in a mesh: tm: 4 (over z), sta: 8 (over y, x, core).
Axes of the slice: x: 2, y: 2, z: 4, core: 2. Of those that a mesh axis runs over, the one named last changes fastest.
Arguments:
- ray_basis: bfloat16 [4, 8192, 256], P('tm', 'sta'), may hold values from -0.13258252 to 0.13258252
- delays: bfloat16 [4, 8192], P('tm', 'sta'), may hold values from -24 to 24
- ray_station: int32 [4, 8192], P('tm', 'sta'), may hold values from 0 to 127, as said below
- ray_count: int32 [4, 8], P('tm', 'sta'), may hold values from 128 to 1024, as said below
- station_var: float32 [128], P('sta'), may hold values from 0.25 to 4
- decay_factor: float32 [4, 256], P('tm'), may hold values from 0.02 to 0.995, as said below
- mode_variance: float32 [256], replicated, may hold values from 0.3 to 3
- prior_mean: float32 [256], replicated, may hold values from -6 to 6
Outputs:
- smoothed: float32 [4, 256], P('tm')
The draws below stay inside these ranges and needn't reach their ends.
Inputs may be any that keep to these rules, and one draw needn't show every extreme that they name: `ray_station`: each ray's station is one of the 16 stations of the station shard that holds the ray. `ray_count`: each entry is a multiple of 128; the live slots of a shard come first; some shard is full in every draw. `decay_factor`: each entry lies strictly between 0 and 1.
All inputs are finite; a program needn't handle non-finite values.
Results may differ from the reference program's by a relative error of at most 0.005.
Values sent between devices are 32-bit elements; how exact they have to be, the bound alone decides.
A program may use at most 64 MiB of HBM per device.

```python
import math
import jax
import jax.numpy as jnp
from jax import lax

STATE = 256
RAY_DEV = 1024
STA_DEV = 16
TOTAL_EPOCHS = 4
RAYS = 8192
STATIONS = 128
STA_SHARDS = 8


def draw_ray_basis(key, part):
    first_key = jax.random.fold_in(jax.random.fold_in(key, 11), 0)
    base = jnp.clip(jax.random.normal(first_key, (TOTAL_EPOCHS, RAYS, STATE), jnp.float32), -6.0, 6.0)
    mixed = base + 0.7 * jnp.roll(base, 1, axis=2) + 0.5 * jnp.roll(base, 7, axis=2)
    return (mixed * (0.45 / math.sqrt(RAYS))).astype(jnp.bfloat16)


def draw_ray_station(key, part):
    local_station = jax.random.randint(jax.random.fold_in(key, 23), (TOTAL_EPOCHS, RAYS), 0, STA_DEV, dtype=jnp.int32)
    shard_index = jnp.arange(RAYS, dtype=jnp.int32) // RAY_DEV
    return shard_index[None, :] * STA_DEV + local_station


def draw_ray_count(key, part):
    divided_keys = jax.random.split(jax.random.fold_in(key, 37), 3)
    blocks = jax.random.randint(divided_keys[0], (TOTAL_EPOCHS, STA_SHARDS), 1, RAY_DEV // 128 + 1, dtype=jnp.int32)
    full_row = jax.random.randint(divided_keys[1], (), 0, TOTAL_EPOCHS, dtype=jnp.int32)
    full_column = jax.random.randint(divided_keys[2], (), 0, STA_SHARDS, dtype=jnp.int32)
    counts = blocks * 128
    return counts.at[full_row, full_column].set(RAY_DEV)


def draw_decay_factor(key, part):
    divided_keys = jax.random.split(jax.random.fold_in(key, 51), 4)
    lowest = math.log(1.0 / (4 * TOTAL_EPOCHS))
    highest = math.log(2.0)
    base_rate = jnp.exp(jax.random.uniform(divided_keys[0], (1, STATE), jnp.float32, lowest, highest))
    factor = jnp.exp(jax.random.uniform(divided_keys[1], (TOTAL_EPOCHS, STATE), jnp.float32, -0.35, 0.35))
    damped_value = jnp.exp(-base_rate * factor)
    outburst_rows = jax.random.randint(divided_keys[2], (3,), 1, TOTAL_EPOCHS, dtype=jnp.int32)
    epoch_position_index = jnp.arange(TOTAL_EPOCHS, dtype=jnp.int32)
    outburst_flag = jnp.any(epoch_position_index[:, None] == outburst_rows[None, :], axis=1)
    outburst_magnitude = jax.random.uniform(divided_keys[3], (TOTAL_EPOCHS, STATE), jnp.float32, 0.5, 0.8)
    return jnp.where(outburst_flag[:, None], damped_value * outburst_magnitude, damped_value)


def level_of(key, extent, pieces, low, largest):
    factor_of = 1.0
    for dim, shards_of in pieces:
        heights = jax.random.uniform(jax.random.fold_in(jax.random.fold_in(key, 6), dim), (shards_of,), jnp.float32, low / len(pieces), largest / len(pieces))
        factor_of = factor_of * jnp.repeat(jnp.exp(heights), extent[dim] // shards_of).reshape((-1,) + (1,) * (len(extent) - 1 - dim))
    return factor_of


def bell_draw(own_key, dims, deviation, most, pieces=(), held_as=jnp.bfloat16):
    drawn = deviation * jax.random.normal(own_key, dims, jnp.float32)
    if pieces:
        drawn = drawn * level_of(own_key, dims, pieces, -0.22, 0.18)
    return jnp.clip(drawn, -most, most).astype(held_as)


def setup_inputs(seed: int = 0) -> dict:
    seeds = jax.random.split(jax.random.key(seed), 9)
    return {
        "ray_basis": draw_ray_basis(jax.random.fold_in(seeds[8], 71), 0),
        "delays": bell_draw(seeds[1], (TOTAL_EPOCHS, RAYS), 4.0, 24.0, ((0, 4), (1, 8))),
        "ray_station": draw_ray_station(jax.random.fold_in(seeds[8], 71), 0),
        "ray_count": draw_ray_count(jax.random.fold_in(seeds[8], 71), 0),
        "station_var": jnp.clip(jnp.exp(math.log(4.0) - 2.7725887 * jax.random.uniform(seeds[4], (STATIONS,), jnp.float32) ** level_of(seeds[4], (STATIONS,), ((0, 8),), -0.2, 0.2)), 0.25, 4.0),
        "decay_factor": draw_decay_factor(jax.random.fold_in(seeds[8], 71), 0),
        "mode_variance": jnp.clip(jnp.exp(jax.random.uniform(seeds[6], (STATE,), jnp.float32, math.log(0.3), math.log(3.0))), 0.3, 3.0),
        "prior_mean": bell_draw(seeds[7], (STATE,), 1.0, 6.0, (), jnp.float32),
    }


PRECISE = lax.Precision.HIGHEST

def product(left, right):
    return jnp.dot(left, right, precision=PRECISE)

def spd_inverse(matrix):
    lower_factor = jnp.linalg.cholesky(matrix)
    identity = jnp.eye(matrix.shape[0], dtype=matrix.dtype)
    inverse = jax.scipy.linalg.cho_solve((lower_factor, True), identity)
    return 0.5 * (inverse + inverse.T)

def kalman_update(mean_prev, info_prev, decay_row, noise_row, information, drive_vector, is_first):
    inverse_noise = 1.0 / noise_row
    scaled = decay_row * inverse_noise
    identity = jnp.eye(noise_row.shape[0], dtype=jnp.float32)
    inner = jnp.where(is_first, identity, info_prev + jnp.diag(decay_row * scaled))
    kernel = spd_inverse(inner)
    pred_info = jnp.diag(inverse_noise) - jnp.where(is_first, 0.0, scaled[:, None] * kernel * scaled[None, :])
    info_new = pred_info + information
    info_new = 0.5 * (info_new + info_new.T)
    target = product(pred_info, decay_row * mean_prev) + drive_vector
    factor = jnp.linalg.cholesky(info_new)
    mean_new = jax.scipy.linalg.cho_solve((factor, True), target)
    return (mean_new, info_new)

def reference(ray_basis, delays, ray_station, ray_count, station_var, decay_factor, mode_variance, prior_mean):
    slot_index = jnp.arange(RAYS, dtype=jnp.int32)
    shard_index = slot_index // RAY_DEV
    within_shard = slot_index - shard_index * RAY_DEV
    process_noise = (1.0 - decay_factor * decay_factor) * mode_variance[None, :]

    def one_epoch(epoch_items):
        basis, delay_row, station_row, count_row = epoch_items
        live_slot = within_shard < count_row[shard_index]
        weight = jnp.where(live_slot, 1.0 / station_var[station_row], 0.0)
        weighted = (basis.astype(jnp.float32) * weight[:, None]).astype(jnp.bfloat16)
        information = jnp.dot(weighted.T.astype(jnp.float32), basis.astype(jnp.float32), preferred_element_type=jnp.float32)
        drive_vector = jnp.dot(delay_row.astype(jnp.float32), weighted.astype(jnp.float32), preferred_element_type=jnp.float32)
        return (information, drive_vector)
    informations, drives = lax.map(one_epoch, (ray_basis, delays, ray_station, ray_count))
    first_flags = jnp.arange(TOTAL_EPOCHS, dtype=jnp.int32) == 0

    def forward(carried, epoch_items):
        information, drive_vector, decay_row, noise_row, is_first = epoch_items
        mean_new, info_new = kalman_update(carried[0], carried[1], decay_row, noise_row, information, drive_vector, is_first)
        return ((mean_new, info_new), (mean_new, info_new))
    start = (prior_mean, jnp.eye(STATE, dtype=jnp.float32))
    _, (filtered, filter_infos) = lax.scan(forward, start, (informations, drives, decay_factor, process_noise, first_flags))
    covariances = lax.map(spd_inverse, filter_infos)

    def backward(adjoint, epoch_items):
        mean_f, cov_f, information, drive_vector, decay_row = epoch_items
        smooth = mean_f + product(cov_f, adjoint)
        adjoint_prev = decay_row * (adjoint + drive_vector - product(information, smooth))
        return (adjoint_prev, smooth)
    _, smoothed = lax.scan(backward, jnp.zeros((STATE,), jnp.float32), (filtered, covariances, informations, drives, decay_factor), reverse=True)
    return smoothed
```

```python
import functools

import jax
import jax.numpy as jnp
from jax import lax
from jax.experimental import pallas as pl
from jax.experimental.pallas import tpu as pltpu
from jax.sharding import PartitionSpec as P

MESH = pl.DeviceIdType.MESH
CORES = 2
TOL = 1e-10
STEPS_PER_CHECK = 4
MAX_CHECKS = 500


def loop(n, body):
    if n <= 16:
        for i in range(n):
            body(i)
    else:
        def step(i, carry):
            body(i)
            return carry

        lax.fori_loop(0, n, step, 0)


def shard_rows(half, shards):
    rows = 3 * half + 2 * (2 * half // 128)
    return -(-rows // (8 * shards)) * 8


def exchange(
    tm_size, sta_size, rows, half,
    basis_ref, delay_ref, station_ref, count_ref, var_ref, decay_ref, out_ref,
    part, landed, rs_send, rs_recv, z_send, plane_send, core_send, gather_recv,
):
    tm = lax.axis_index("tm")
    sta = lax.axis_index("sta")
    core = sta % CORES
    chip = sta // CORES
    chips = sta_size // CORES

    barrier = pltpu.get_barrier_semaphore()

    def greet_plane(i):
        peer = (sta + 1 + i) % sta_size
        pl.semaphore_signal(barrier, inc=1, device_id=(tm, peer), device_id_type=MESH)

    def greet_column(i):
        peer = (tm + 1 + i) % tm_size
        pl.semaphore_signal(barrier, inc=1, device_id=(peer, sta), device_id_type=MESH)

    loop(sta_size - 1, greet_plane)
    loop(tm_size - 1, greet_column)

    rays = basis_ref.shape[1]
    width = 2 * half
    groups = rays // 128
    local = station_ref[...] - sta * var_ref.shape[0]
    slots = lax.broadcasted_iota(jnp.int32, (1, rays), 1)
    weight = jnp.zeros((1, rays), jnp.float32)
    for s in range(var_ref.shape[0]):
        value = jnp.full((1, rays), var_ref[s], jnp.float32)
        weight = jnp.where(local == s, 1.0 / value, weight)
    weight = jnp.where(slots < count_ref[0, 0], weight, 0.0)
    square = jnp.concatenate(
        [weight[:, g * 128 : (g + 1) * 128] for g in range(groups)]
        + [jnp.zeros((128 - groups, 128), jnp.float32)],
        axis=0,
    )
    columns = square.T
    weighted = jnp.concatenate(
        [
            (basis_ref[0, g * 128 : (g + 1) * 128, :].astype(jnp.float32) * columns[:, g : g + 1])
            for g in range(groups)
        ],
        axis=0,
    ).astype(jnp.bfloat16)
    basis = basis_ref[0]
    outer = (((0,), (0,)), ((), ()))
    left = lax.dot_general(
        weighted, basis[:, :half], outer, preferred_element_type=jnp.float32
    )
    corner = lax.dot_general(
        weighted[:, half:], basis[:, half:], outer, preferred_element_type=jnp.float32
    )
    drive = jnp.dot(delay_ref[...], weighted, preferred_element_type=jnp.float32)
    keep = jnp.where(jnp.full((1, width), sta, jnp.int32) == 0, decay_ref[...], 0.0)
    tail = [drive[:, i * half : (i + 1) * half] for i in range(2)]
    tail += [keep[:, i * half : (i + 1) * half] for i in range(2)]
    pad = sta_size * rows - 3 * half - 4
    flat = jnp.concatenate(
        [left, corner] + tail + [jnp.zeros((pad, half), jnp.float32)], axis=0
    )
    for s in range(sta_size):
        part[s] = flat[s * rows : (s + 1) * rows]

    pl.semaphore_wait(barrier, sta_size + tm_size - 2)

    def scatter(i):
        peer = (sta + 1 + i) % sta_size
        return pltpu.make_async_remote_copy(
            src_ref=part.at[peer], dst_ref=landed.at[sta],
            send_sem=rs_send.at[i], recv_sem=rs_recv.at[sta],
            device_id=(tm, peer), device_id_type=MESH,
        )

    def scattered(i):
        peer = (sta + 1 + i) % sta_size
        return pltpu.make_async_remote_copy(
            src_ref=part.at[peer], dst_ref=landed.at[peer],
            send_sem=rs_send.at[i], recv_sem=rs_recv.at[peer],
            device_id=(tm, peer), device_id_type=MESH,
        )

    loop(sta_size - 1, lambda i: scatter(i).start())
    loop(sta_size - 1, lambda i: scattered(i).wait_recv())
    total = part[sta]
    if sta_size <= 16:
        for i in range(sta_size - 1):
            total = total + landed[(sta + 1 + i) % sta_size]
    else:
        total = lax.fori_loop(
            0, sta_size - 1, lambda i, t: t + landed[(sta + 1 + i) % sta_size], total
        )
    out_ref[tm, sta] = total

    def slot_copy(z, s, send_sem, device):
        return pltpu.make_async_remote_copy(
            src_ref=out_ref.at[z, s], dst_ref=out_ref.at[z, s],
            send_sem=send_sem, recv_sem=gather_recv.at[z, s],
            device_id=device, device_id_type=MESH,
        )

    def column_copy(i):
        return slot_copy(tm, sta, z_send.at[i], ((tm + 1 + i) % tm_size, sta))

    def plane_copy(z, i):
        peer = ((chip + 1 + i) % chips) * CORES + core
        return slot_copy(z, sta, plane_send.at[z, i], (tm, peer))

    def core_copy(z, c):
        return slot_copy(z, c * CORES + core, core_send.at[z, c], (tm, chip * CORES + 1 - core))

    def spread(z):
        loop(chips - 1, lambda i: plane_copy(z, i).start())
        core_copy(z, chip).start()

    loop(tm_size - 1, lambda i: column_copy(i).start())
    spread(tm)

    def relay(i):
        z = (tm + 1 + i) % tm_size
        slot_copy(z, sta, core_send.at[z, chip], (tm, sta)).wait_recv()
        spread(z)

    loop(tm_size - 1, relay)

    def share(j):
        z = (tm + j) % tm_size

        def one(i):
            c = (chip + 1 + i) % chips
            slot_copy(z, c * CORES + core, core_send.at[z, c], (tm, sta)).wait_recv()
            core_copy(z, c).start()

        loop(chips - 1, one)

    loop(tm_size, share)

    def collect(z):
        def one(c):
            slot_copy(
                z, c * CORES + 1 - core, core_send.at[z, c], (tm, sta)
            ).wait_recv()

        loop(chips, one)

    loop(tm_size, collect)
    loop(sta_size - 1, lambda i: scatter(i).wait_send())
    loop(tm_size - 1, lambda i: column_copy(i).wait_send())

    def drain(z):
        loop(chips - 1, lambda i: plane_copy(z, i).wait_send())
        loop(chips, lambda c: core_copy(z, c).wait_send())

    loop(tm_size, drain)


def total_of(rows):
    acc = rows[0]
    for row in rows[1:]:
        acc = acc + row
    return jnp.sum(acc, axis=1, keepdims=True)


def solve(epochs, half, packed_ref, variance_ref, prior_ref, out_ref, table):
    width = 2 * half
    tm = lax.axis_index("tm")
    row_id = lax.broadcasted_iota(jnp.int32, (half, half), 0)
    col_id = lax.broadcasted_iota(jnp.int32, (half, half), 1)
    diagonal = row_id == col_id
    variance = variance_ref[...]
    decay, drive, info_diag = [], [], []
    for e in range(epochs):
        upper = packed_ref[e, :half]
        lower = packed_ref[e, half : 2 * half]
        corner = packed_ref[e, 2 * half : 3 * half]
        matrix = jnp.concatenate(
            [
                jnp.concatenate([upper, lower.T], axis=1),
                jnp.concatenate([lower, corner], axis=1),
            ],
            axis=0,
        )
        high = matrix.astype(jnp.bfloat16)
        table[e, :width] = high
        table[e, width:] = (matrix - high.astype(jnp.float32)).astype(jnp.bfloat16)
        info_diag.append(
            jnp.concatenate(
                [
                    jnp.sum(jnp.where(diagonal, block, 0.0), axis=0, keepdims=True)
                    for block in (upper, corner)
                ],
                axis=1,
            )
        )
        tail = packed_ref[e, 3 * half : 3 * half + 8]
        drive.append(jnp.concatenate([tail[0:1], tail[1:2]], axis=1))
        decay.append(jnp.concatenate([tail[2:3], tail[3:4]], axis=1))
    inverse_noise = [1.0 / ((1.0 - d * d) * variance) for d in decay]
    off = [-decay[e] * inverse_noise[e] for e in range(epochs)]
    main = []
    for e in range(epochs):
        value = inverse_noise[e]
        if e + 1 < epochs:
            value = value + decay[e + 1] * decay[e + 1] * inverse_noise[e + 1]
        main.append(value)
    target = list(drive)
    target[0] = target[0] + inverse_noise[0] * (decay[0] * prior_ref[...])

    pivot_inverse, ratio = [], []
    for e in range(epochs):
        pivot = main[e] + info_diag[e]
        if e:
            ratio.append(off[e] * pivot_inverse[-1])
            pivot = pivot - ratio[-1] * off[e]
        pivot_inverse.append(1.0 / pivot)

    def precondition(r):
        y = [r[0]]
        for e in range(1, epochs):
            y.append(r[e] - ratio[e - 1] * y[-1])
        z = [None] * epochs
        z[-1] = y[-1] * pivot_inverse[-1]
        for e in range(epochs - 2, -1, -1):
            z[e] = y[e] * pivot_inverse[e] - ratio[e] * z[e + 1]
        return z

    pick = lax.broadcasted_iota(jnp.int32, (8, width), 0)

    def apply(p):
        result = []
        for e in range(epochs):
            first = p[e].astype(jnp.bfloat16).astype(jnp.float32)
            rest = p[e] - first
            second = rest.astype(jnp.bfloat16).astype(jnp.float32)
            third = rest - second
            stacked = jnp.where(
                pick == 0, first, jnp.where(pick == 1, second, jnp.where(pick == 2, third, 0.0))
            ).astype(jnp.bfloat16)
            both = jnp.concatenate([stacked, stacked], axis=1)
            product = jnp.dot(both, table[e], preferred_element_type=jnp.float32)
            value = main[e] * p[e] + jnp.sum(product, axis=0, keepdims=True)
            if e:
                value = value + off[e] * p[e - 1]
            if e + 1 < epochs:
                value = value + off[e + 1] * p[e + 1]
            result.append(value)
        return result

    tiny = 1e-30
    zero = [jnp.zeros((1, width), jnp.float32)] * epochs
    first_z = precondition(target)
    first_rz = total_of([a * b for a, b in zip(target, first_z)])
    goal = TOL * first_rz

    def body(carry):
        count, _, x, r, p, rz = carry
        x, r, p = list(x), list(r), list(p)
        for _ in range(STEPS_PER_CHECK):
            q = apply(p)
            bend = total_of([a * b for a, b in zip(p, q)])
            alpha = rz / jnp.maximum(bend, tiny)
            x = [a + alpha * b for a, b in zip(x, p)]
            r = [a - alpha * b for a, b in zip(r, q)]
            z = precondition(r)
            new = total_of([a * b for a, b in zip(r, z)])
            beta = new / jnp.maximum(rz, tiny)
            p = [a + beta * b for a, b in zip(z, p)]
            rz = new
        going = jnp.max((rz > goal).astype(jnp.int32)) > 0
        return (count + 1, going, tuple(x), tuple(r), tuple(p), rz)

    start = (
        jnp.int32(0), jnp.max((first_rz > tiny).astype(jnp.int32)) > 0,
        tuple(zero), tuple(target), tuple(first_z), first_rz,
    )
    final = lax.while_loop(lambda c: jnp.logical_and(c[1], c[0] < MAX_CHECKS), body, start)
    chosen = final[2][0]
    for e in range(1, epochs):
        chosen = jnp.where(tm == e, final[2][e], chosen)
    out_ref[...] = chosen


def shards(
    ray_basis, delays, ray_station, ray_count, station_var, decay_factor, mode_variance, prior_mean
):
    tm_size = lax.axis_size("tm")
    sta_size = lax.axis_size("sta")
    width = ray_basis.shape[2]
    half = width // 2
    rows = shard_rows(half, sta_size)
    chips = sta_size // CORES
    vmem = pl.BlockSpec(memory_space=pltpu.VMEM)
    smem = pl.BlockSpec(memory_space=pltpu.SMEM)
    dma = pltpu.SemaphoreType.DMA
    packed = pl.pallas_call(
        functools.partial(exchange, tm_size, sta_size, rows, half),
        out_shape=jax.ShapeDtypeStruct((tm_size, sta_size, rows, half), jnp.float32),
        in_specs=[vmem, vmem, vmem, smem, smem, vmem],
        out_specs=vmem,
        scratch_shapes=[
            pltpu.VMEM((sta_size, rows, half), jnp.float32),
            pltpu.VMEM((sta_size, rows, half), jnp.float32),
            dma((sta_size - 1,)),
            dma((sta_size,)),
            dma((tm_size - 1,)),
            dma((tm_size, chips - 1)),
            dma((tm_size, chips)),
            dma((tm_size, sta_size)),
        ],
        compiler_params=pltpu.CompilerParams(collective_id=0, has_side_effects=True),
        name="exchange",
    )(ray_basis, delays, ray_station, ray_count, station_var, decay_factor)
    packed = packed.reshape(tm_size, sta_size * rows, half)
    return pl.pallas_call(
        functools.partial(solve, tm_size, half),
        out_shape=jax.ShapeDtypeStruct((1, width), jnp.float32),
        in_specs=[vmem, vmem, vmem],
        out_specs=vmem,
        scratch_shapes=[pltpu.VMEM((tm_size, 2 * width, width), jnp.bfloat16)],
        name="solve",
    )(packed, mode_variance.reshape(1, width), prior_mean.reshape(1, width))


def solution(mesh):
    placed = (
        P("tm", "sta", None),
        P("tm", "sta"),
        P("tm", "sta"),
        P("tm", "sta"),
        P("sta"),
        P("tm", None),
        P(),
        P(),
    )
    return jax.shard_map(
        shards, mesh=mesh, in_specs=placed, out_specs=P("tm", None), check_vma=False
    )
```

```python
import functools

import jax
import jax.numpy as jnp
from jax import lax
from jax.experimental import pallas as pl
from jax.experimental.pallas import tpu as pltpu
from jax.sharding import PartitionSpec as P

MESH = pl.DeviceIdType.MESH
CORES = 2
TOL = 2e-8
FIRST_STEPS = 7
STEPS_PER_CHECK = 3
MAX_CHECKS = 700
VMEM_BYTES = 24 << 20


def loop(n, body):
    if n <= 16:
        for i in range(n):
            body(i)
    else:
        def step(i, carry):
            body(i)
            return carry

        lax.fori_loop(0, n, step, 0)


def shard_rows(half, shards):
    rows = 2 * half + 5
    return -(-rows // (8 * shards)) * 8


def exchange(
    tm_size, sta_size, rows, half,
    basis_ref, delay_ref, station_ref, count_ref, var_ref, decay_ref, out_ref,
    part, landed, rs_send, rs_recv, z_send, plane_send, core_send, gather_recv,
):
    tm = lax.axis_index("tm")
    sta = lax.axis_index("sta")
    core = sta % CORES
    chip = sta // CORES
    chips = sta_size // CORES

    barrier = pltpu.get_barrier_semaphore()

    def greet_plane(i):
        peer = (sta + 1 + i) % sta_size
        pl.semaphore_signal(barrier, inc=1, device_id=(tm, peer), device_id_type=MESH)

    def greet_column(i):
        peer = (tm + 1 + i) % tm_size
        pl.semaphore_signal(barrier, inc=1, device_id=(peer, sta), device_id_type=MESH)

    loop(sta_size - 1, greet_plane)
    loop(tm_size - 1, greet_column)

    rays = basis_ref.shape[1]
    width = 2 * half
    groups = rays // 128
    local = station_ref[...] - sta * var_ref.shape[0]
    slots = lax.broadcasted_iota(jnp.int32, (1, rays), 1)
    noise = jnp.ones((1, rays), jnp.float32)
    for s in range(var_ref.shape[0]):
        noise = jnp.where(local == s, var_ref[s], noise)
    weight = jnp.where(slots < count_ref[0, 0], 1.0 / noise, 0.0)
    square = jnp.concatenate(
        [weight[:, g * 128 : (g + 1) * 128] for g in range(groups)]
        + [jnp.zeros((128 - groups, 128), jnp.float32)],
        axis=0,
    )
    columns = square.T
    weighted = jnp.concatenate(
        [
            (basis_ref[0, g * 128 : (g + 1) * 128, :].astype(jnp.float32) * columns[:, g : g + 1])
            for g in range(groups)
        ],
        axis=0,
    ).astype(jnp.bfloat16)
    basis = basis_ref[0]
    outer = (((0,), (0,)), ((), ()))
    left = lax.dot_general(
        weighted, basis[:, :half], outer, preferred_element_type=jnp.float32
    )
    corner = lax.dot_general(
        weighted[:, half:], basis[:, half:], outer, preferred_element_type=jnp.float32
    )
    drive = jnp.dot(delay_ref[...], weighted, preferred_element_type=jnp.float32)
    keep = jnp.where(jnp.full((1, width), sta, jnp.int32) == 0, decay_ref[...], 0.0)
    row_id = lax.broadcasted_iota(jnp.int32, (half, half), 0)
    col_id = lax.broadcasted_iota(jnp.int32, (half, half), 1)
    mixed = jnp.where(row_id >= col_id, left[:half], corner)
    tail = [jnp.sum(jnp.where(row_id == col_id, corner, 0.0), axis=0, keepdims=True)]
    tail += [drive[:, i * half : (i + 1) * half] for i in range(2)]
    tail += [keep[:, i * half : (i + 1) * half] for i in range(2)]
    pad = sta_size * rows - 2 * half - 5
    flat = jnp.concatenate(
        [mixed, left[half:]] + tail + [jnp.zeros((pad, half), jnp.float32)], axis=0
    )
    for s in range(sta_size):
        part[s] = flat[s * rows : (s + 1) * rows]

    pl.semaphore_wait(barrier, sta_size + tm_size - 2)

    def scatter(i):
        peer = (sta + 1 + i) % sta_size
        return pltpu.make_async_remote_copy(
            src_ref=part.at[peer], dst_ref=landed.at[sta],
            send_sem=rs_send.at[i], recv_sem=rs_recv.at[sta],
            device_id=(tm, peer), device_id_type=MESH,
        )

    def scattered(i):
        peer = (sta + 1 + i) % sta_size
        return pltpu.make_async_remote_copy(
            src_ref=part.at[peer], dst_ref=landed.at[peer],
            send_sem=rs_send.at[i], recv_sem=rs_recv.at[peer],
            device_id=(tm, peer), device_id_type=MESH,
        )

    loop(sta_size - 1, lambda i: scatter(i).start())
    loop(sta_size - 1, lambda i: scattered(i).wait_recv())
    total = part[sta]
    if sta_size <= 16:
        for i in range(sta_size - 1):
            total = total + landed[(sta + 1 + i) % sta_size]
    else:
        total = lax.fori_loop(
            0, sta_size - 1, lambda i, t: t + landed[(sta + 1 + i) % sta_size], total
        )
    out_ref[tm, sta] = total

    def slot_copy(z, s, send_sem, device):
        return pltpu.make_async_remote_copy(
            src_ref=out_ref.at[z, s], dst_ref=out_ref.at[z, s],
            send_sem=send_sem, recv_sem=gather_recv.at[z, s],
            device_id=device, device_id_type=MESH,
        )

    def column_copy(i):
        return slot_copy(tm, sta, z_send.at[i], ((tm + 1 + i) % tm_size, sta))

    def plane_copy(z, i):
        peer = ((chip + 1 + i) % chips) * CORES + core
        return slot_copy(z, sta, plane_send.at[z, i], (tm, peer))

    def core_copy(z, c):
        return slot_copy(z, c * CORES + core, core_send.at[z, c], (tm, chip * CORES + 1 - core))

    def spread(z):
        loop(chips - 1, lambda i: plane_copy(z, i).start())
        core_copy(z, chip).start()

    loop(tm_size - 1, lambda i: column_copy(i).start())
    spread(tm)

    def relay(i):
        z = (tm + 1 + i) % tm_size
        slot_copy(z, sta, core_send.at[z, chip], (tm, sta)).wait_recv()
        spread(z)

    loop(tm_size - 1, relay)

    def share(j):
        z = (tm + j) % tm_size

        def one(i):
            c = (chip + 1 + i) % chips
            slot_copy(z, c * CORES + core, core_send.at[z, c], (tm, sta)).wait_recv()
            core_copy(z, c).start()

        loop(chips - 1, one)

    loop(tm_size, share)

    def collect(z):
        def one(c):
            slot_copy(
                z, c * CORES + 1 - core, core_send.at[z, c], (tm, sta)
            ).wait_recv()

        loop(chips, one)

    loop(tm_size, collect)
    loop(sta_size - 1, lambda i: scatter(i).wait_send())
    loop(tm_size - 1, lambda i: column_copy(i).wait_send())

    def drain(z):
        loop(chips - 1, lambda i: plane_copy(z, i).wait_send())
        loop(chips, lambda c: core_copy(z, c).wait_send())

    loop(tm_size, drain)


def total_of(rows):
    acc = rows[0]
    for row in rows[1:]:
        acc = acc + row
    return jnp.sum(acc, axis=1, keepdims=True)


def solve(epochs, half, packed_ref, variance_ref, prior_ref, out_ref, table):
    width = 2 * half
    tm = lax.axis_index("tm")
    row_id = lax.broadcasted_iota(jnp.int32, (half, half), 0)
    col_id = lax.broadcasted_iota(jnp.int32, (half, half), 1)
    diagonal = row_id == col_id
    variance = variance_ref[...]
    decay, drive, info_diag = [], [], []
    for e in range(epochs):
        mixed = packed_ref[e, :half]
        lower = packed_ref[e, half : 2 * half]
        tail = packed_ref[e, 2 * half : 2 * half + 8]
        flipped = mixed.T
        upper = jnp.where(row_id >= col_id, mixed, flipped)
        corner = jnp.where(
            row_id < col_id, mixed, jnp.where(diagonal, tail[0:1], flipped)
        )
        matrix = jnp.concatenate(
            [
                jnp.concatenate([upper, lower.T], axis=1),
                jnp.concatenate([lower, corner], axis=1),
            ],
            axis=0,
        )
        high = matrix.astype(jnp.bfloat16)
        table[e, :width] = high
        table[e, width:] = (matrix - high.astype(jnp.float32)).astype(jnp.bfloat16)
        info_diag.append(
            jnp.concatenate(
                [jnp.sum(jnp.where(diagonal, mixed, 0.0), axis=0, keepdims=True), tail[0:1]],
                axis=1,
            )
        )
        drive.append(jnp.concatenate([tail[1:2], tail[2:3]], axis=1))
        decay.append(jnp.concatenate([tail[3:4], tail[4:5]], axis=1))
    inverse_noise = [1.0 / ((1.0 - d * d) * variance) for d in decay]
    off = [-decay[e] * inverse_noise[e] for e in range(epochs)]
    main = []
    for e in range(epochs):
        value = inverse_noise[e]
        if e + 1 < epochs:
            value = value + decay[e + 1] * decay[e + 1] * inverse_noise[e + 1]
        main.append(value)
    target = list(drive)
    target[0] = target[0] + inverse_noise[0] * (decay[0] * prior_ref[...])

    pivot_inverse, ratio = [], []
    for e in range(epochs):
        pivot = main[e] + info_diag[e]
        if e:
            ratio.append(off[e] * pivot_inverse[-1])
            pivot = pivot - ratio[-1] * off[e]
        pivot_inverse.append(1.0 / pivot)

    def precondition(r):
        y = [r[0]]
        for e in range(1, epochs):
            y.append(r[e] - ratio[e - 1] * y[-1])
        z = [None] * epochs
        z[-1] = y[-1] * pivot_inverse[-1]
        for e in range(epochs - 2, -1, -1):
            z[e] = y[e] * pivot_inverse[e] - ratio[e] * z[e + 1]
        return z

    pick = lax.broadcasted_iota(jnp.int32, (8, width), 0)

    def apply(p):
        result = []
        for e in range(epochs):
            first = p[e].astype(jnp.bfloat16).astype(jnp.float32)
            rest = p[e] - first
            second = rest.astype(jnp.bfloat16).astype(jnp.float32)
            third = rest - second
            stacked = jnp.where(
                pick == 0, first, jnp.where(pick == 1, second, jnp.where(pick == 2, third, 0.0))
            ).astype(jnp.bfloat16)
            both = jnp.concatenate([stacked, stacked], axis=1)
            product = jnp.dot(both, table[e], preferred_element_type=jnp.float32)
            value = main[e] * p[e] + jnp.sum(product, axis=0, keepdims=True)
            if e:
                value = value + off[e] * p[e - 1]
            if e + 1 < epochs:
                value = value + off[e + 1] * p[e + 1]
            result.append(value)
        return result

    tiny = 1e-30
    zero = [jnp.zeros((1, width), jnp.float32)] * epochs
    first_z = precondition(target)
    first_rz = total_of([a * b for a, b in zip(target, first_z)])
    goal = TOL * first_rz

    def advance(state, steps):
        x, r, p, rz = list(state[0]), list(state[1]), list(state[2]), state[3]
        for _ in range(steps):
            q = apply(p)
            bend = total_of([a * b for a, b in zip(p, q)])
            alpha = rz / jnp.maximum(bend, tiny)
            x = [a + alpha * b for a, b in zip(x, p)]
            r = [a - alpha * b for a, b in zip(r, q)]
            z = precondition(r)
            new = total_of([a * b for a, b in zip(r, z)])
            beta = new / jnp.maximum(rz, tiny)
            p = [a + beta * b for a, b in zip(z, p)]
            rz = new
        return tuple(x), tuple(r), tuple(p), rz

    def going(rz):
        return jnp.max((rz > goal).astype(jnp.int32)) > 0

    def body(carry):
        count, _, state = carry
        state = advance(state, STEPS_PER_CHECK)
        return count + 1, going(state[3]), state

    state = advance((zero, target, first_z, first_rz), FIRST_STEPS)
    final = lax.while_loop(
        lambda c: jnp.logical_and(c[1], c[0] < MAX_CHECKS),
        body,
        (jnp.int32(0), going(state[3]), state),
    )[2][0]
    chosen = final[0]
    for e in range(1, epochs):
        chosen = jnp.where(tm == e, final[e], chosen)
    out_ref[...] = chosen


def shards(
    ray_basis, delays, ray_station, ray_count, station_var, decay_factor, mode_variance, prior_mean
):
    tm_size = lax.axis_size("tm")
    sta_size = lax.axis_size("sta")
    width = ray_basis.shape[2]
    half = width // 2
    rows = shard_rows(half, sta_size)
    chips = sta_size // CORES
    vmem = pl.BlockSpec(memory_space=pltpu.VMEM)
    smem = pl.BlockSpec(memory_space=pltpu.SMEM)
    dma = pltpu.SemaphoreType.DMA
    packed = pl.pallas_call(
        functools.partial(exchange, tm_size, sta_size, rows, half),
        out_shape=jax.ShapeDtypeStruct((tm_size, sta_size, rows, half), jnp.float32),
        in_specs=[vmem, vmem, vmem, smem, smem, vmem],
        out_specs=vmem,
        scratch_shapes=[
            pltpu.VMEM((sta_size, rows, half), jnp.float32),
            pltpu.VMEM((sta_size, rows, half), jnp.float32),
            dma((sta_size - 1,)),
            dma((sta_size,)),
            dma((tm_size - 1,)),
            dma((tm_size, chips - 1)),
            dma((tm_size, chips)),
            dma((tm_size, sta_size)),
        ],
        compiler_params=pltpu.CompilerParams(
            collective_id=0, has_side_effects=True, vmem_limit_bytes=VMEM_BYTES
        ),
        name="exchange",
    )(ray_basis, delays, ray_station, ray_count, station_var, decay_factor)
    packed = packed.reshape(tm_size, sta_size * rows, half)
    return pl.pallas_call(
        functools.partial(solve, tm_size, half),
        out_shape=jax.ShapeDtypeStruct((1, width), jnp.float32),
        in_specs=[vmem, vmem, vmem],
        out_specs=vmem,
        scratch_shapes=[pltpu.VMEM((tm_size, 2 * width, width), jnp.bfloat16)],
        compiler_params=pltpu.CompilerParams(vmem_limit_bytes=VMEM_BYTES),
        name="solve",
    )(packed, mode_variance.reshape(1, width), prior_mean.reshape(1, width))


def solution(mesh):
    placed = (
        P("tm", "sta", None),
        P("tm", "sta"),
        P("tm", "sta"),
        P("tm", "sta"),
        P("sta"),
        P("tm", None),
        P(),
        P(),
    )
    return jax.shard_map(
        shards, mesh=mesh, in_specs=placed, out_specs=P("tm", None), check_vma=False
    )
```

```python
import functools

import jax
import jax.numpy as jnp
from jax import lax
from jax.experimental import pallas as pl
from jax.experimental.pallas import tpu as pltpu
from jax.sharding import PartitionSpec as P

MESH = pl.DeviceIdType.MESH
CORES = 2
TOL = 2e-8
FIRST_STEPS = 7
STEPS_PER_CHECK = 3
MAX_CHECKS = 700
VMEM_BYTES = 24 << 20


def loop(n, body):
    if n <= 16:
        for i in range(n):
            body(i)
    else:
        def step(i, carry):
            body(i)
            return carry

        lax.fori_loop(0, n, step, 0)


def shard_rows(half, shards):
    rows = 2 * half + 5
    return -(-rows // (8 * shards)) * 8


def exchange(
    tm_size, sta_size, rows, half,
    basis_hbm, delay_hbm, station_hbm, count_hbm, var_hbm, decay_hbm, out_ref,
    basis_ref, delay_ref, station_ref, count_ref, var_ref, decay_ref, load_sem,
    part, landed, rs_send, rs_recv, z_send, plane_send, core_send, gather_recv, chain,
):
    tm = lax.axis_index("tm")
    sta = lax.axis_index("sta")
    core = sta % CORES
    chip = sta // CORES
    chips = sta_size // CORES

    barrier = pltpu.get_barrier_semaphore()

    def greet_plane(i):
        peer = (sta + 1 + i) % sta_size
        pl.semaphore_signal(barrier, inc=1, device_id=(tm, peer), device_id_type=MESH)

    has_below, has_above = tm > 0, tm < tm_size - 1

    def to_neighbours(below_sem, above_sem):
        @pl.when(has_below)
        def _():
            pl.semaphore_signal(
                below_sem, inc=1, device_id=(tm - 1, sta), device_id_type=MESH
            )

        @pl.when(has_above)
        def _():
            pl.semaphore_signal(
                above_sem, inc=1, device_id=(tm + 1, sta), device_id_type=MESH
            )

    to_neighbours(barrier, barrier)
    loop(sta_size - 1, greet_plane)

    loads = [
        pltpu.make_async_copy(source, target, load_sem.at[i])
        for i, (source, target) in enumerate(
            (
                (count_hbm, count_ref), (var_hbm, var_ref), (station_hbm, station_ref),
                (basis_hbm, basis_ref), (delay_hbm, delay_ref), (decay_hbm, decay_ref),
            )
        )
    ]
    for load in loads:
        load.start()
    for load in loads:
        load.wait()

    rays = basis_ref.shape[1]
    width = 2 * half
    groups = rays // 128
    local = station_ref[...] - sta * var_ref.shape[0]
    slots = lax.broadcasted_iota(jnp.int32, (1, rays), 1)
    noise = jnp.ones((1, rays), jnp.float32)
    for s in range(var_ref.shape[0]):
        noise = jnp.where(local == s, var_ref[s], noise)
    weight = jnp.where(slots < count_ref[0, 0], 1.0 / noise, 0.0)
    square = jnp.concatenate(
        [weight[:, g * 128 : (g + 1) * 128] for g in range(groups)]
        + [jnp.zeros((128 - groups, 128), jnp.float32)],
        axis=0,
    )
    columns = square.T
    weighted = jnp.concatenate(
        [
            (basis_ref[0, g * 128 : (g + 1) * 128, :].astype(jnp.float32) * columns[:, g : g + 1])
            for g in range(groups)
        ],
        axis=0,
    ).astype(jnp.bfloat16)
    basis = basis_ref[0]
    outer = (((0,), (0,)), ((), ()))
    left = lax.dot_general(
        weighted, basis[:, :half], outer, preferred_element_type=jnp.float32
    )
    corner = lax.dot_general(
        weighted[:, half:], basis[:, half:], outer, preferred_element_type=jnp.float32
    )
    drive = jnp.dot(delay_ref[...], weighted, preferred_element_type=jnp.float32)
    keep = jnp.where(jnp.full((1, width), sta, jnp.int32) == 0, decay_ref[...], 0.0)
    row_id = lax.broadcasted_iota(jnp.int32, (half, half), 0)
    col_id = lax.broadcasted_iota(jnp.int32, (half, half), 1)
    mixed = jnp.where(row_id >= col_id, left[:half], corner)
    tail = [jnp.sum(jnp.where(row_id == col_id, corner, 0.0), axis=0, keepdims=True)]
    tail += [drive[:, i * half : (i + 1) * half] for i in range(2)]
    tail += [keep[:, i * half : (i + 1) * half] for i in range(2)]
    pad = sta_size * rows - 2 * half - 5
    flat = jnp.concatenate(
        [mixed, left[half:]] + tail + [jnp.zeros((pad, half), jnp.float32)], axis=0
    )
    for s in range(sta_size):
        part[s] = flat[s * rows : (s + 1) * rows]

    pl.semaphore_wait(
        barrier, sta_size - 1 + has_below.astype(jnp.int32) + has_above.astype(jnp.int32)
    )

    def scatter(i):
        peer = (sta + 1 + i) % sta_size
        return pltpu.make_async_remote_copy(
            src_ref=part.at[peer], dst_ref=landed.at[sta],
            send_sem=rs_send.at[i], recv_sem=rs_recv.at[sta],
            device_id=(tm, peer), device_id_type=MESH,
        )

    def scattered(i):
        peer = (sta + 1 + i) % sta_size
        return pltpu.make_async_remote_copy(
            src_ref=part.at[peer], dst_ref=landed.at[peer],
            send_sem=rs_send.at[i], recv_sem=rs_recv.at[peer],
            device_id=(tm, peer), device_id_type=MESH,
        )

    loop(sta_size - 1, lambda i: scatter(i).start())

    def widen(i):
        to_neighbours(chain.at[0], chain.at[1])

        @pl.when(has_above)
        def _():
            pl.semaphore_wait(chain.at[0], 1)

        @pl.when(has_below)
        def _():
            pl.semaphore_wait(chain.at[1], 1)

    loop(tm_size - 2, widen)
    loop(sta_size - 1, lambda i: scattered(i).wait_recv())
    total = part[sta]
    if sta_size <= 16:
        for i in range(sta_size - 1):
            total = total + landed[(sta + 1 + i) % sta_size]
    else:
        total = lax.fori_loop(
            0, sta_size - 1, lambda i, t: t + landed[(sta + 1 + i) % sta_size], total
        )
    out_ref[tm, sta] = total

    def slot_copy(z, s, send_sem, device):
        return pltpu.make_async_remote_copy(
            src_ref=out_ref.at[z, s], dst_ref=out_ref.at[z, s],
            send_sem=send_sem, recv_sem=gather_recv.at[z, s],
            device_id=device, device_id_type=MESH,
        )

    def column_copy(i):
        return slot_copy(tm, sta, z_send.at[i], ((tm + 1 + i) % tm_size, sta))

    def plane_copy(z, i):
        peer = ((chip + 1 + i) % chips) * CORES + core
        return slot_copy(z, sta, plane_send.at[z, i], (tm, peer))

    def core_copy(z, c):
        return slot_copy(z, c * CORES + core, core_send.at[z, c], (tm, chip * CORES + 1 - core))

    def spread(z):
        loop(chips - 1, lambda i: plane_copy(z, i).start())
        core_copy(z, chip).start()

    loop(tm_size - 1, lambda i: column_copy(i).start())
    spread(tm)

    def relay(i):
        z = (tm + 1 + i) % tm_size
        slot_copy(z, sta, core_send.at[z, chip], (tm, sta)).wait_recv()
        spread(z)

    loop(tm_size - 1, relay)

    def share(j):
        z = (tm + j) % tm_size

        def one(i):
            c = (chip + 1 + i) % chips
            slot_copy(z, c * CORES + core, core_send.at[z, c], (tm, sta)).wait_recv()
            core_copy(z, c).start()

        loop(chips - 1, one)

    loop(tm_size, share)

    def collect(z):
        def one(c):
            slot_copy(
                z, c * CORES + 1 - core, core_send.at[z, c], (tm, sta)
            ).wait_recv()

        loop(chips, one)

    loop(tm_size, collect)
    loop(sta_size - 1, lambda i: scatter(i).wait_send())
    loop(tm_size - 1, lambda i: column_copy(i).wait_send())

    def drain(z):
        loop(chips - 1, lambda i: plane_copy(z, i).wait_send())
        loop(chips, lambda c: core_copy(z, c).wait_send())

    loop(tm_size, drain)


def total_of(rows):
    acc = rows[0]
    for row in rows[1:]:
        acc = acc + row
    return jnp.sum(acc, axis=1, keepdims=True)


def solve(
    epochs, half, packed_ref, variance_hbm, prior_hbm, out_ref,
    table, variance_ref, prior_ref, load_sem,
):
    loads = [
        pltpu.make_async_copy(variance_hbm, variance_ref, load_sem.at[0]),
        pltpu.make_async_copy(prior_hbm, prior_ref, load_sem.at[1]),
    ]
    for load in loads:
        load.start()
    width = 2 * half
    tm = lax.axis_index("tm")
    row_id = lax.broadcasted_iota(jnp.int32, (half, half), 0)
    col_id = lax.broadcasted_iota(jnp.int32, (half, half), 1)
    diagonal = row_id == col_id
    decay, drive, info_diag = [], [], []
    for e in range(epochs):
        mixed = packed_ref[e, :half]
        lower = packed_ref[e, half : 2 * half]
        tail = packed_ref[e, 2 * half : 2 * half + 8]
        flipped = mixed.T
        upper = jnp.where(row_id >= col_id, mixed, flipped)
        corner = jnp.where(
            row_id < col_id, mixed, jnp.where(diagonal, tail[0:1], flipped)
        )
        matrix = jnp.concatenate(
            [
                jnp.concatenate([upper, lower.T], axis=1),
                jnp.concatenate([lower, corner], axis=1),
            ],
            axis=0,
        )
        high = matrix.astype(jnp.bfloat16)
        table[e, :width] = high
        table[e, width:] = (matrix - high.astype(jnp.float32)).astype(jnp.bfloat16)
        info_diag.append(
            jnp.concatenate(
                [jnp.sum(jnp.where(diagonal, mixed, 0.0), axis=0, keepdims=True), tail[0:1]],
                axis=1,
            )
        )
        drive.append(jnp.concatenate([tail[1:2], tail[2:3]], axis=1))
        decay.append(jnp.concatenate([tail[3:4], tail[4:5]], axis=1))
    for load in loads:
        load.wait()
    variance = variance_ref[...]
    inverse_noise = [1.0 / ((1.0 - d * d) * variance) for d in decay]
    off = [-decay[e] * inverse_noise[e] for e in range(epochs)]
    main = []
    for e in range(epochs):
        value = inverse_noise[e]
        if e + 1 < epochs:
            value = value + decay[e + 1] * decay[e + 1] * inverse_noise[e + 1]
        main.append(value)
    target = list(drive)
    target[0] = target[0] + inverse_noise[0] * (decay[0] * prior_ref[...])

    pivot_inverse, ratio = [], []
    for e in range(epochs):
        pivot = main[e] + info_diag[e]
        if e:
            ratio.append(off[e] * pivot_inverse[-1])
            pivot = pivot - ratio[-1] * off[e]
        pivot_inverse.append(1.0 / pivot)

    def precondition(r):
        y = [r[0]]
        for e in range(1, epochs):
            y.append(r[e] - ratio[e - 1] * y[-1])
        z = [None] * epochs
        z[-1] = y[-1] * pivot_inverse[-1]
        for e in range(epochs - 2, -1, -1):
            z[e] = y[e] * pivot_inverse[e] - ratio[e] * z[e + 1]
        return z

    pick = lax.broadcasted_iota(jnp.int32, (8, width), 0)

    def apply(p):
        result = []
        for e in range(epochs):
            first = p[e].astype(jnp.bfloat16).astype(jnp.float32)
            rest = p[e] - first
            second = rest.astype(jnp.bfloat16).astype(jnp.float32)
            third = rest - second
            stacked = jnp.where(
                pick == 0, first, jnp.where(pick == 1, second, jnp.where(pick == 2, third, 0.0))
            ).astype(jnp.bfloat16)
            both = jnp.concatenate([stacked, stacked], axis=1)
            product = jnp.dot(both, table[e], preferred_element_type=jnp.float32)
            value = main[e] * p[e] + jnp.sum(product, axis=0, keepdims=True)
            if e:
                value = value + off[e] * p[e - 1]
            if e + 1 < epochs:
                value = value + off[e + 1] * p[e + 1]
            result.append(value)
        return result

    tiny = 1e-30
    zero = [jnp.zeros((1, width), jnp.float32)] * epochs
    first_z = precondition(target)
    first_rz = total_of([a * b for a, b in zip(target, first_z)])
    goal = TOL * first_rz

    def advance(state, steps):
        x, r, p, rz = list(state[0]), list(state[1]), list(state[2]), state[3]
        for _ in range(steps):
            q = apply(p)
            bend = total_of([a * b for a, b in zip(p, q)])
            alpha = rz / jnp.maximum(bend, tiny)
            x = [a + alpha * b for a, b in zip(x, p)]
            r = [a - alpha * b for a, b in zip(r, q)]
            z = precondition(r)
            new = total_of([a * b for a, b in zip(r, z)])
            beta = new / jnp.maximum(rz, tiny)
            p = [a + beta * b for a, b in zip(z, p)]
            rz = new
        return tuple(x), tuple(r), tuple(p), rz

    def going(rz):
        return jnp.max((rz > goal).astype(jnp.int32)) > 0

    def body(carry):
        count, _, state = carry
        state = advance(state, STEPS_PER_CHECK)
        return count + 1, going(state[3]), state

    state = advance((zero, target, first_z, first_rz), FIRST_STEPS)
    final = lax.while_loop(
        lambda c: jnp.logical_and(c[1], c[0] < MAX_CHECKS),
        body,
        (jnp.int32(0), going(state[3]), state),
    )[2][0]
    chosen = final[0]
    for e in range(1, epochs):
        chosen = jnp.where(tm == e, final[e], chosen)
    out_ref[...] = chosen


def shards(
    ray_basis, delays, ray_station, ray_count, station_var, decay_factor, mode_variance, prior_mean
):
    tm_size = lax.axis_size("tm")
    sta_size = lax.axis_size("sta")
    width = ray_basis.shape[2]
    half = width // 2
    rows = shard_rows(half, sta_size)
    chips = sta_size // CORES
    vmem = pl.BlockSpec(memory_space=pltpu.VMEM)
    hbm = pl.BlockSpec(memory_space=pltpu.HBM)
    dma = pltpu.SemaphoreType.DMA
    packed = pl.pallas_call(
        functools.partial(exchange, tm_size, sta_size, rows, half),
        out_shape=jax.ShapeDtypeStruct((tm_size, sta_size, rows, half), jnp.float32),
        in_specs=[hbm] * 6,
        out_specs=vmem,
        scratch_shapes=[
            pltpu.VMEM(ray_basis.shape, ray_basis.dtype),
            pltpu.VMEM(delays.shape, delays.dtype),
            pltpu.VMEM(ray_station.shape, ray_station.dtype),
            pltpu.SMEM(ray_count.shape, ray_count.dtype),
            pltpu.SMEM(station_var.shape, station_var.dtype),
            pltpu.VMEM(decay_factor.shape, decay_factor.dtype),
            dma((6,)),
            pltpu.VMEM((sta_size, rows, half), jnp.float32),
            pltpu.VMEM((sta_size, rows, half), jnp.float32),
            dma((sta_size - 1,)),
            dma((sta_size,)),
            dma((tm_size - 1,)),
            dma((tm_size, chips - 1)),
            dma((tm_size, chips)),
            dma((tm_size, sta_size)),
            pltpu.SemaphoreType.REGULAR((2,)),
        ],
        compiler_params=pltpu.CompilerParams(
            collective_id=0, has_side_effects=True, vmem_limit_bytes=VMEM_BYTES
        ),
        name="exchange",
    )(*[
        pltpu.with_memory_space_constraint(x, pltpu.HBM)
        for x in (ray_basis, delays, ray_station)
    ], ray_count, *[
        pltpu.with_memory_space_constraint(x, pltpu.HBM) for x in (station_var, decay_factor)
    ])
    packed = packed.reshape(tm_size, sta_size * rows, half)
    return pl.pallas_call(
        functools.partial(solve, tm_size, half),
        out_shape=jax.ShapeDtypeStruct((1, width), jnp.float32),
        in_specs=[vmem, hbm, hbm],
        out_specs=vmem,
        scratch_shapes=[
            pltpu.VMEM((tm_size, 2 * width, width), jnp.bfloat16),
            pltpu.VMEM((1, width), jnp.float32),
            pltpu.VMEM((1, width), jnp.float32),
            dma((2,)),
        ],
        compiler_params=pltpu.CompilerParams(vmem_limit_bytes=VMEM_BYTES),
        name="solve",
    )(packed, *[
        pltpu.with_memory_space_constraint(x.reshape(1, width), pltpu.HBM)
        for x in (mode_variance, prior_mean)
    ])


def solution(mesh):
    placed = (
        P("tm", "sta", None),
        P("tm", "sta"),
        P("tm", "sta"),
        P("tm", "sta"),
        P("sta"),
        P("tm", None),
        P(),
        P(),
    )
    return jax.shard_map(
        shards, mesh=mesh, in_specs=placed, out_specs=P("tm", None), check_vma=False
    )
```

```python
import functools

import jax
import jax.numpy as jnp
from jax import lax
from jax.experimental import pallas as pl
from jax.experimental.pallas import tpu as pltpu
from jax.sharding import PartitionSpec as P

MESH = pl.DeviceIdType.MESH
CORES = 2
TOL = 2e-8
FIRST_STEPS = 7
STEPS_PER_CHECK = 3
MAX_CHECKS = 700
VMEM_BYTES = 24 << 20


def loop(n, body):
    if n <= 16:
        for i in range(n):
            body(i)
    else:
        def step(i, carry):
            body(i)
            return carry

        lax.fori_loop(0, n, step, 0)


def shard_rows(half, shards):
    rows = 2 * half + 5
    return -(-rows // (8 * shards)) * 8


def exchange(
    tm_size, sta_size, rows, half,
    basis_hbm, delay_hbm, station_hbm, count_ref, var_hbm, decay_hbm, variance_hbm, prior_hbm,
    out_ref, variance_ref, prior_ref,
    basis_ref, delay_ref, station_ref, var_ref, decay_ref, load_sem,
    part, landed, rs_send, rs_recv, z_send, plane_send, core_send, gather_recv, chain,
):
    tm = lax.axis_index("tm")
    sta = lax.axis_index("sta")
    core = sta % CORES
    chip = sta // CORES
    chips = sta_size // CORES

    barrier = pltpu.get_barrier_semaphore()

    def greet_plane(i):
        peer = (sta + 1 + i) % sta_size
        pl.semaphore_signal(barrier, inc=1, device_id=(tm, peer), device_id_type=MESH)

    has_below, has_above = tm > 0, tm < tm_size - 1

    def to_neighbours(below_sem, above_sem):
        @pl.when(has_below)
        def _():
            pl.semaphore_signal(
                below_sem, inc=1, device_id=(tm - 1, sta), device_id_type=MESH
            )

        @pl.when(has_above)
        def _():
            pl.semaphore_signal(
                above_sem, inc=1, device_id=(tm + 1, sta), device_id_type=MESH
            )

    to_neighbours(barrier, barrier)
    loop(sta_size - 1, greet_plane)

    loads = [
        pltpu.make_async_copy(source, target, load_sem.at[i])
        for i, (source, target) in enumerate(
            (
                (var_hbm, var_ref), (station_hbm, station_ref),
                (basis_hbm, basis_ref), (delay_hbm, delay_ref), (decay_hbm, decay_ref),
                (variance_hbm, variance_ref), (prior_hbm, prior_ref),
            )
        )
    ]
    for load in loads:
        load.start()
    for load in loads:
        load.wait()

    rays = basis_ref.shape[1]
    width = 2 * half
    groups = rays // 128
    local = station_ref[...] - sta * var_ref.shape[0]
    slots = lax.broadcasted_iota(jnp.int32, (1, rays), 1)
    noise = jnp.ones((1, rays), jnp.float32)
    for s in range(var_ref.shape[0]):
        noise = jnp.where(local == s, var_ref[s], noise)
    weight = jnp.where(slots < count_ref[...], 1.0 / noise, 0.0)
    square = jnp.concatenate(
        [weight[:, g * 128 : (g + 1) * 128] for g in range(groups)]
        + [jnp.zeros((128 - groups, 128), jnp.float32)],
        axis=0,
    )
    columns = square.T
    weighted = jnp.concatenate(
        [
            (basis_ref[0, g * 128 : (g + 1) * 128, :].astype(jnp.float32) * columns[:, g : g + 1])
            for g in range(groups)
        ],
        axis=0,
    ).astype(jnp.bfloat16)
    basis = basis_ref[0]
    outer = (((0,), (0,)), ((), ()))
    left = lax.dot_general(
        weighted, basis[:, :half], outer, preferred_element_type=jnp.float32
    )
    corner = lax.dot_general(
        weighted[:, half:], basis[:, half:], outer, preferred_element_type=jnp.float32
    )
    drive = jnp.dot(delay_ref[...], weighted, preferred_element_type=jnp.float32)
    keep = jnp.where(jnp.full((1, width), sta, jnp.int32) == 0, decay_ref[...], 0.0)
    row_id = lax.broadcasted_iota(jnp.int32, (half, half), 0)
    col_id = lax.broadcasted_iota(jnp.int32, (half, half), 1)
    mixed = jnp.where(row_id >= col_id, left[:half], corner)
    tail = [jnp.sum(jnp.where(row_id == col_id, corner, 0.0), axis=0, keepdims=True)]
    tail += [drive[:, i * half : (i + 1) * half] for i in range(2)]
    tail += [keep[:, i * half : (i + 1) * half] for i in range(2)]
    pad = sta_size * rows - 2 * half - 5
    flat = jnp.concatenate(
        [mixed, left[half:]] + tail + [jnp.zeros((pad, half), jnp.float32)], axis=0
    )
    for s in range(sta_size):
        part[s] = flat[s * rows : (s + 1) * rows]

    pl.semaphore_wait(
        barrier, sta_size - 1 + has_below.astype(jnp.int32) + has_above.astype(jnp.int32)
    )

    def scatter(i):
        peer = (sta + 1 + i) % sta_size
        return pltpu.make_async_remote_copy(
            src_ref=part.at[peer], dst_ref=landed.at[sta],
            send_sem=rs_send.at[i], recv_sem=rs_recv.at[sta],
            device_id=(tm, peer), device_id_type=MESH,
        )

    def scattered(i):
        peer = (sta + 1 + i) % sta_size
        return pltpu.make_async_remote_copy(
            src_ref=part.at[peer], dst_ref=landed.at[peer],
            send_sem=rs_send.at[i], recv_sem=rs_recv.at[peer],
            device_id=(tm, peer), device_id_type=MESH,
        )

    loop(sta_size - 1, lambda i: scatter(i).start())

    def widen(i):
        to_neighbours(chain.at[0], chain.at[1])

        @pl.when(has_above)
        def _():
            pl.semaphore_wait(chain.at[0], 1)

        @pl.when(has_below)
        def _():
            pl.semaphore_wait(chain.at[1], 1)

    loop(tm_size - 2, widen)
    loop(sta_size - 1, lambda i: scattered(i).wait_recv())
    total = part[sta]
    if sta_size <= 16:
        for i in range(sta_size - 1):
            total = total + landed[(sta + 1 + i) % sta_size]
    else:
        total = lax.fori_loop(
            0, sta_size - 1, lambda i, t: t + landed[(sta + 1 + i) % sta_size], total
        )
    out_ref[tm, sta] = total

    def slot_copy(z, s, send_sem, device):
        return pltpu.make_async_remote_copy(
            src_ref=out_ref.at[z, s], dst_ref=out_ref.at[z, s],
            send_sem=send_sem, recv_sem=gather_recv.at[z, s],
            device_id=device, device_id_type=MESH,
        )

    def column_copy(i):
        return slot_copy(tm, sta, z_send.at[i], ((tm + 1 + i) % tm_size, sta))

    def plane_copy(z, i):
        peer = ((chip + 1 + i) % chips) * CORES + core
        return slot_copy(z, sta, plane_send.at[z, i], (tm, peer))

    def core_copy(z, c):
        return slot_copy(z, c * CORES + core, core_send.at[z, c], (tm, chip * CORES + 1 - core))

    def spread(z):
        loop(chips - 1, lambda i: plane_copy(z, i).start())
        core_copy(z, chip).start()

    loop(tm_size - 1, lambda i: column_copy(i).start())
    spread(tm)

    def relay(i):
        z = (tm + 1 + i) % tm_size
        slot_copy(z, sta, core_send.at[z, chip], (tm, sta)).wait_recv()
        spread(z)

    loop(tm_size - 1, relay)

    def share(j):
        z = (tm + j) % tm_size

        def one(i):
            c = (chip + 1 + i) % chips
            slot_copy(z, c * CORES + core, core_send.at[z, c], (tm, sta)).wait_recv()
            core_copy(z, c).start()

        loop(chips - 1, one)

    loop(tm_size, share)

    def collect(z):
        def one(c):
            slot_copy(
                z, c * CORES + 1 - core, core_send.at[z, c], (tm, sta)
            ).wait_recv()

        loop(chips, one)

    loop(tm_size, collect)
    loop(sta_size - 1, lambda i: scatter(i).wait_send())
    loop(tm_size - 1, lambda i: column_copy(i).wait_send())

    def drain(z):
        loop(chips - 1, lambda i: plane_copy(z, i).wait_send())
        loop(chips, lambda c: core_copy(z, c).wait_send())

    loop(tm_size, drain)


def total_of(rows):
    acc = rows[0]
    for row in rows[1:]:
        acc = acc + row
    return jnp.sum(acc, axis=1, keepdims=True)


def solve(epochs, half, packed_ref, variance_ref, prior_ref, out_ref, table):
    width = 2 * half
    tm = lax.axis_index("tm")
    row_id = lax.broadcasted_iota(jnp.int32, (half, half), 0)
    col_id = lax.broadcasted_iota(jnp.int32, (half, half), 1)
    diagonal = row_id == col_id
    decay, drive, info_diag = [], [], []
    for e in range(epochs):
        mixed = packed_ref[e, :half]
        lower = packed_ref[e, half : 2 * half]
        tail = packed_ref[e, 2 * half : 2 * half + 8]
        flipped = mixed.T
        upper = jnp.where(row_id >= col_id, mixed, flipped)
        corner = jnp.where(
            row_id < col_id, mixed, jnp.where(diagonal, tail[0:1], flipped)
        )
        matrix = jnp.concatenate(
            [
                jnp.concatenate([upper, lower.T], axis=1),
                jnp.concatenate([lower, corner], axis=1),
            ],
            axis=0,
        )
        high = matrix.astype(jnp.bfloat16)
        table[e, :width] = high
        table[e, width:] = (matrix - high.astype(jnp.float32)).astype(jnp.bfloat16)
        info_diag.append(
            jnp.concatenate(
                [jnp.sum(jnp.where(diagonal, mixed, 0.0), axis=0, keepdims=True), tail[0:1]],
                axis=1,
            )
        )
        drive.append(jnp.concatenate([tail[1:2], tail[2:3]], axis=1))
        decay.append(jnp.concatenate([tail[3:4], tail[4:5]], axis=1))
    variance = variance_ref[...]
    inverse_noise = [1.0 / ((1.0 - d * d) * variance) for d in decay]
    off = [-decay[e] * inverse_noise[e] for e in range(epochs)]
    main = []
    for e in range(epochs):
        value = inverse_noise[e]
        if e + 1 < epochs:
            value = value + decay[e + 1] * decay[e + 1] * inverse_noise[e + 1]
        main.append(value)
    target = list(drive)
    target[0] = target[0] + inverse_noise[0] * (decay[0] * prior_ref[...])

    pivot_inverse, ratio = [], []
    for e in range(epochs):
        pivot = main[e] + info_diag[e]
        if e:
            ratio.append(off[e] * pivot_inverse[-1])
            pivot = pivot - ratio[-1] * off[e]
        pivot_inverse.append(1.0 / pivot)

    def precondition(r):
        y = [r[0]]
        for e in range(1, epochs):
            y.append(r[e] - ratio[e - 1] * y[-1])
        z = [None] * epochs
        z[-1] = y[-1] * pivot_inverse[-1]
        for e in range(epochs - 2, -1, -1):
            z[e] = y[e] * pivot_inverse[e] - ratio[e] * z[e + 1]
        return z

    pick = lax.broadcasted_iota(jnp.int32, (8, width), 0)

    def apply(p):
        result = []
        for e in range(epochs):
            first = p[e].astype(jnp.bfloat16).astype(jnp.float32)
            rest = p[e] - first
            second = rest.astype(jnp.bfloat16).astype(jnp.float32)
            third = rest - second
            stacked = jnp.where(
                pick == 0, first, jnp.where(pick == 1, second, jnp.where(pick == 2, third, 0.0))
            ).astype(jnp.bfloat16)
            both = jnp.concatenate([stacked, stacked], axis=1)
            product = jnp.dot(both, table[e], preferred_element_type=jnp.float32)
            value = main[e] * p[e] + jnp.sum(product, axis=0, keepdims=True)
            if e:
                value = value + off[e] * p[e - 1]
            if e + 1 < epochs:
                value = value + off[e + 1] * p[e + 1]
            result.append(value)
        return result

    tiny = 1e-30
    zero = [jnp.zeros((1, width), jnp.float32)] * epochs
    first_z = precondition(target)
    first_rz = total_of([a * b for a, b in zip(target, first_z)])
    goal = TOL * first_rz

    def advance(state, steps):
        x, r, p, rz = list(state[0]), list(state[1]), list(state[2]), state[3]
        for _ in range(steps):
            q = apply(p)
            bend = total_of([a * b for a, b in zip(p, q)])
            alpha = rz / jnp.maximum(bend, tiny)
            x = [a + alpha * b for a, b in zip(x, p)]
            r = [a - alpha * b for a, b in zip(r, q)]
            z = precondition(r)
            new = total_of([a * b for a, b in zip(r, z)])
            beta = new / jnp.maximum(rz, tiny)
            p = [a + beta * b for a, b in zip(z, p)]
            rz = new
        return tuple(x), tuple(r), tuple(p), rz

    def going(rz):
        return jnp.max((rz > goal).astype(jnp.int32)) > 0

    def body(carry):
        count, _, state = carry
        state = advance(state, STEPS_PER_CHECK)
        return count + 1, going(state[3]), state

    state = advance((zero, target, first_z, first_rz), FIRST_STEPS)
    final = lax.while_loop(
        lambda c: jnp.logical_and(c[1], c[0] < MAX_CHECKS),
        body,
        (jnp.int32(0), going(state[3]), state),
    )[2][0]
    chosen = final[0]
    for e in range(1, epochs):
        chosen = jnp.where(tm == e, final[e], chosen)
    out_ref[...] = chosen


def shards(
    ray_basis, delays, ray_station, ray_count, station_var, decay_factor, mode_variance, prior_mean
):
    tm_size = lax.axis_size("tm")
    sta_size = lax.axis_size("sta")
    width = ray_basis.shape[2]
    half = width // 2
    rows = shard_rows(half, sta_size)
    chips = sta_size // CORES
    vmem = pl.BlockSpec(memory_space=pltpu.VMEM)
    hbm = pl.BlockSpec(memory_space=pltpu.HBM)
    dma = pltpu.SemaphoreType.DMA
    packed, variance, prior = pl.pallas_call(
        functools.partial(exchange, tm_size, sta_size, rows, half),
        out_shape=(
            jax.ShapeDtypeStruct((tm_size, sta_size, rows, half), jnp.float32),
            jax.ShapeDtypeStruct((1, width), jnp.float32),
            jax.ShapeDtypeStruct((1, width), jnp.float32),
        ),
        in_specs=[hbm, hbm, hbm, vmem, hbm, hbm, hbm, hbm],
        out_specs=(vmem, vmem, vmem),
        scratch_shapes=[
            pltpu.VMEM(ray_basis.shape, ray_basis.dtype),
            pltpu.VMEM(delays.shape, delays.dtype),
            pltpu.VMEM(ray_station.shape, ray_station.dtype),
            pltpu.SMEM(station_var.shape, station_var.dtype),
            pltpu.VMEM(decay_factor.shape, decay_factor.dtype),
            dma((7,)),
            pltpu.VMEM((sta_size, rows, half), jnp.float32),
            pltpu.VMEM((sta_size, rows, half), jnp.float32),
            dma((sta_size - 1,)),
            dma((sta_size,)),
            dma((tm_size - 1,)),
            dma((tm_size, chips - 1)),
            dma((tm_size, chips)),
            dma((tm_size, sta_size)),
            pltpu.SemaphoreType.REGULAR((2,)),
        ],
        compiler_params=pltpu.CompilerParams(
            collective_id=0, has_side_effects=True, vmem_limit_bytes=VMEM_BYTES
        ),
        name="exchange",
    )(*[
        pltpu.with_memory_space_constraint(x, pltpu.HBM)
        for x in (ray_basis, delays, ray_station)
    ], ray_count, *[
        pltpu.with_memory_space_constraint(x, pltpu.HBM) for x in (
            station_var, decay_factor,
            mode_variance.reshape(1, width), prior_mean.reshape(1, width),
        )
    ])
    packed = packed.reshape(tm_size, sta_size * rows, half)
    return pl.pallas_call(
        functools.partial(solve, tm_size, half),
        out_shape=jax.ShapeDtypeStruct((1, width), jnp.float32),
        in_specs=[vmem, vmem, vmem],
        out_specs=vmem,
        scratch_shapes=[
            pltpu.VMEM((tm_size, 2 * width, width), jnp.bfloat16),
        ],
        compiler_params=pltpu.CompilerParams(vmem_limit_bytes=VMEM_BYTES),
        name="solve",
    )(packed, variance, prior)


def solution(mesh):
    placed = (
        P("tm", "sta", None),
        P("tm", "sta"),
        P("tm", "sta"),
        P("tm", "sta"),
        P("sta"),
        P("tm", None),
        P(),
        P(),
    )
    return jax.shard_map(
        shards, mesh=mesh, in_specs=placed, out_specs=P("tm", None), check_vma=False
    )
```

```python
import functools

import jax
import jax.numpy as jnp
from jax import lax
from jax.experimental import pallas as pl
from jax.experimental.pallas import tpu as pltpu
from jax.sharding import PartitionSpec as P

MESH = pl.DeviceIdType.MESH
CORES = 2
TOL = 2e-8
FIRST_STEPS = 7
STEPS_PER_CHECK = 3
MAX_CHECKS = 700
VMEM_BYTES = 24 << 20


def loop(n, body):
    if n <= 16:
        for i in range(n):
            body(i)
    else:
        def step(i, carry):
            body(i)
            return carry

        lax.fori_loop(0, n, step, 0)


def shard_rows(half, shards):
    rows = 2 * half + 5
    return -(-rows // (8 * shards)) * 8


def exchange(
    tm_size, sta_size, rows, half,
    basis_hbm, delay_hbm, station_hbm, count_ref, var_hbm, decay_hbm, variance_hbm, prior_hbm,
    out_ref, variance_ref, prior_ref,
    basis_ref, delay_ref, station_ref, var_ref, decay_ref, load_sem,
    part, landed, rs_send, rs_recv, z_send, plane_send, core_send, gather_recv, chain,
):
    tm = lax.axis_index("tm")
    sta = lax.axis_index("sta")
    core = sta % CORES
    chip = sta // CORES
    chips = sta_size // CORES

    barrier = pltpu.get_barrier_semaphore()

    def greet_plane(i):
        peer = (sta + 1 + i) % sta_size
        pl.semaphore_signal(barrier, inc=1, device_id=(tm, peer), device_id_type=MESH)

    has_below, has_above = tm > 0, tm < tm_size - 1

    def to_neighbours(below_sem, above_sem):
        @pl.when(has_below)
        def _():
            pl.semaphore_signal(
                below_sem, inc=1, device_id=(tm - 1, sta), device_id_type=MESH
            )

        @pl.when(has_above)
        def _():
            pl.semaphore_signal(
                above_sem, inc=1, device_id=(tm + 1, sta), device_id_type=MESH
            )

    to_neighbours(barrier, barrier)
    loop(sta_size - 1, greet_plane)

    loads = [
        pltpu.make_async_copy(source, target, load_sem.at[i])
        for i, (source, target) in enumerate(
            (
                (var_hbm, var_ref), (station_hbm, station_ref),
                (basis_hbm, basis_ref), (delay_hbm, delay_ref), (decay_hbm, decay_ref),
                (variance_hbm, variance_ref), (prior_hbm, prior_ref),
            )
        )
    ]
    for load in loads:
        load.start()
    for load in loads:
        load.wait()

    rays = basis_ref.shape[1]
    width = 2 * half
    groups = rays // 128
    local = station_ref[...] - sta * var_ref.shape[0]
    slots = lax.broadcasted_iota(jnp.int32, (1, rays), 1)
    noise = jnp.ones((1, rays), jnp.float32)
    for s in range(var_ref.shape[0]):
        noise = jnp.where(local == s, var_ref[s], noise)
    weight = jnp.where(slots < count_ref[...], 1.0 / noise, 0.0)
    square = jnp.concatenate(
        [weight[:, g * 128 : (g + 1) * 128] for g in range(groups)]
        + [jnp.zeros((128 - groups, 128), jnp.float32)],
        axis=0,
    )
    columns = square.T
    weighted = jnp.concatenate(
        [
            (basis_ref[0, g * 128 : (g + 1) * 128, :].astype(jnp.float32) * columns[:, g : g + 1])
            for g in range(groups)
        ],
        axis=0,
    ).astype(jnp.bfloat16)
    basis = basis_ref[0]
    outer = (((0,), (0,)), ((), ()))
    left = lax.dot_general(
        weighted, basis[:, :half], outer, preferred_element_type=jnp.float32
    )
    corner = lax.dot_general(
        weighted[:, half:], basis[:, half:], outer, preferred_element_type=jnp.float32
    )
    drive = jnp.dot(delay_ref[...], weighted, preferred_element_type=jnp.float32)
    keep = jnp.where(jnp.full((1, width), sta, jnp.int32) == 0, decay_ref[...], 0.0)
    row_id = lax.broadcasted_iota(jnp.int32, (half, half), 0)
    col_id = lax.broadcasted_iota(jnp.int32, (half, half), 1)
    mixed = jnp.where(row_id >= col_id, left[:half], corner)
    tail = [jnp.sum(jnp.where(row_id == col_id, corner, 0.0), axis=0, keepdims=True)]
    tail += [drive[:, i * half : (i + 1) * half] for i in range(2)]
    tail += [keep[:, i * half : (i + 1) * half] for i in range(2)]
    pad = sta_size * rows - 2 * half - 5
    flat = jnp.concatenate(
        [mixed, left[half:]] + tail + [jnp.zeros((pad, half), jnp.float32)], axis=0
    )
    for s in range(sta_size):
        part[s] = flat[s * rows : (s + 1) * rows]

    pl.semaphore_wait(
        barrier, sta_size - 1 + has_below.astype(jnp.int32) + has_above.astype(jnp.int32)
    )

    def scatter(i):
        peer = (sta + 1 + i) % sta_size
        return pltpu.make_async_remote_copy(
            src_ref=part.at[peer], dst_ref=landed.at[sta],
            send_sem=rs_send.at[i], recv_sem=rs_recv.at[sta],
            device_id=(tm, peer), device_id_type=MESH,
        )

    def scattered(i):
        peer = (sta + 1 + i) % sta_size
        return pltpu.make_async_remote_copy(
            src_ref=part.at[peer], dst_ref=landed.at[peer],
            send_sem=rs_send.at[i], recv_sem=rs_recv.at[peer],
            device_id=(tm, peer), device_id_type=MESH,
        )

    loop(sta_size - 1, lambda i: scatter(i).start())

    def widen(i):
        to_neighbours(chain.at[0], chain.at[1])

        @pl.when(has_above)
        def _():
            pl.semaphore_wait(chain.at[0], 1)

        @pl.when(has_below)
        def _():
            pl.semaphore_wait(chain.at[1], 1)

    loop(tm_size - 2, widen)
    loop(sta_size - 1, lambda i: scattered(i).wait_recv())
    total = part[sta]
    if sta_size <= 16:
        for i in range(sta_size - 1):
            total = total + landed[(sta + 1 + i) % sta_size]
    else:
        total = lax.fori_loop(
            0, sta_size - 1, lambda i, t: t + landed[(sta + 1 + i) % sta_size], total
        )
    out_ref[tm, sta] = total

    def slot_copy(z, s, send_sem, device):
        return pltpu.make_async_remote_copy(
            src_ref=out_ref.at[z, s], dst_ref=out_ref.at[z, s],
            send_sem=send_sem, recv_sem=gather_recv.at[z, s],
            device_id=device, device_id_type=MESH,
        )

    def column_copy(i):
        return slot_copy(tm, sta, z_send.at[i], ((tm + 1 + i) % tm_size, sta))

    def plane_copy(z, i):
        peer = ((chip + 1 + i) % chips) * CORES + core
        return slot_copy(z, sta, plane_send.at[z, i], (tm, peer))

    def core_copy(z, c):
        return slot_copy(z, c * CORES + core, core_send.at[z, c], (tm, chip * CORES + 1 - core))

    def spread(z):
        loop(chips - 1, lambda i: plane_copy(z, i).start())
        core_copy(z, chip).start()

    loop(tm_size - 1, lambda i: column_copy(i).start())
    spread(tm)

    def relay(i):
        z = (tm + 1 + i) % tm_size
        slot_copy(z, sta, core_send.at[z, chip], (tm, sta)).wait_recv()
        spread(z)

    loop(tm_size - 1, relay)

    def share(j):
        z = (tm + j) % tm_size

        def one(i):
            c = (chip + 1 + i) % chips
            slot_copy(z, c * CORES + core, core_send.at[z, c], (tm, sta)).wait_recv()
            core_copy(z, c).start()

        loop(chips - 1, one)

    loop(tm_size, share)

    def collect(z):
        def one(c):
            slot_copy(
                z, c * CORES + 1 - core, core_send.at[z, c], (tm, sta)
            ).wait_recv()

        loop(chips, one)

    loop(tm_size, collect)
    loop(sta_size - 1, lambda i: scatter(i).wait_send())
    loop(tm_size - 1, lambda i: column_copy(i).wait_send())

    def drain(z):
        loop(chips - 1, lambda i: plane_copy(z, i).wait_send())
        loop(chips, lambda c: core_copy(z, c).wait_send())

    loop(tm_size, drain)


def total_of(rows):
    acc = rows[0]
    for row in rows[1:]:
        acc = acc + row
    return jnp.sum(acc, axis=1, keepdims=True)


def solve(epochs, half, packed_ref, variance_ref, prior_ref, out_ref, table):
    width = 2 * half
    tm = lax.axis_index("tm")
    row_id = lax.broadcasted_iota(jnp.int32, (half, half), 0)
    col_id = lax.broadcasted_iota(jnp.int32, (half, half), 1)
    diagonal = row_id == col_id
    decay, drive, info_diag = [], [], []
    for e in range(epochs):
        mixed = packed_ref[e, :half]
        lower = packed_ref[e, half : 2 * half]
        tail = packed_ref[e, 2 * half : 2 * half + 8]
        flipped = mixed.T
        upper = jnp.where(row_id >= col_id, mixed, flipped)
        corner = jnp.where(
            row_id < col_id, mixed, jnp.where(diagonal, tail[0:1], flipped)
        )
        matrix = jnp.concatenate(
            [
                jnp.concatenate([upper, lower.T], axis=1),
                jnp.concatenate([lower, corner], axis=1),
            ],
            axis=0,
        )
        high = matrix.astype(jnp.bfloat16)
        table[e, :width] = high
        table[e, width:] = (matrix - high.astype(jnp.float32)).astype(jnp.bfloat16)
        info_diag.append(
            jnp.concatenate(
                [jnp.sum(jnp.where(diagonal, mixed, 0.0), axis=0, keepdims=True), tail[0:1]],
                axis=1,
            )
        )
        drive.append(jnp.concatenate([tail[1:2], tail[2:3]], axis=1))
        decay.append(jnp.concatenate([tail[3:4], tail[4:5]], axis=1))
    variance = variance_ref[...]
    inverse_noise = [1.0 / ((1.0 - d * d) * variance) for d in decay]
    off = [-decay[e] * inverse_noise[e] for e in range(epochs)]
    main = []
    for e in range(epochs):
        value = inverse_noise[e]
        if e + 1 < epochs:
            value = value + decay[e + 1] * decay[e + 1] * inverse_noise[e + 1]
        main.append(value)
    target = list(drive)
    target[0] = target[0] + inverse_noise[0] * (decay[0] * prior_ref[...])

    pivot_inverse, ratio = [], []
    for e in range(epochs):
        pivot = main[e] + info_diag[e]
        if e:
            ratio.append(off[e] * pivot_inverse[-1])
            pivot = pivot - ratio[-1] * off[e]
        pivot_inverse.append(1.0 / pivot)

    def precondition(r):
        y = [r[0]]
        for e in range(1, epochs):
            y.append(r[e] - ratio[e - 1] * y[-1])
        z = [None] * epochs
        z[-1] = y[-1] * pivot_inverse[-1]
        for e in range(epochs - 2, -1, -1):
            z[e] = y[e] * pivot_inverse[e] - ratio[e] * z[e + 1]
        return z

    pick = lax.broadcasted_iota(jnp.int32, (8, width), 0)

    def apply(p):
        result = []
        for e in range(epochs):
            first = p[e].astype(jnp.bfloat16).astype(jnp.float32)
            rest = p[e] - first
            second = rest.astype(jnp.bfloat16).astype(jnp.float32)
            third = rest - second
            stacked = jnp.where(
                pick == 0, first, jnp.where(pick == 1, second, jnp.where(pick == 2, third, 0.0))
            ).astype(jnp.bfloat16)
            both = jnp.concatenate([stacked, stacked], axis=1)
            product = jnp.dot(both, table[e], preferred_element_type=jnp.float32)
            value = main[e] * p[e] + jnp.sum(product, axis=0, keepdims=True)
            if e:
                value = value + off[e] * p[e - 1]
            if e + 1 < epochs:
                value = value + off[e + 1] * p[e + 1]
            result.append(value)
        return result

    tiny = 1e-30
    zero = [jnp.zeros((1, width), jnp.float32)] * epochs
    first_z = precondition(target)
    first_rz = total_of([a * b for a, b in zip(target, first_z)])
    goal = TOL * first_rz

    def advance(state, steps):
        x, r, p, rz = list(state[0]), list(state[1]), list(state[2]), state[3]
        for _ in range(steps):
            q = apply(p)
            bend = total_of([a * b for a, b in zip(p, q)])
            alpha = rz / jnp.maximum(bend, tiny)
            x = [a + alpha * b for a, b in zip(x, p)]
            r = [a - alpha * b for a, b in zip(r, q)]
            z = precondition(r)
            new = total_of([a * b for a, b in zip(r, z)])
            beta = new / jnp.maximum(rz, tiny)
            p = [a + beta * b for a, b in zip(z, p)]
            rz = new
        return tuple(x), tuple(r), tuple(p), rz

    def opening(x, r, u, gamma):
        w = apply(u)
        alpha = gamma / jnp.maximum(total_of([a * b for a, b in zip(u, w)]), tiny)
        p, s = u, w
        for step in range(FIRST_STEPS):
            x = [a + alpha * b for a, b in zip(x, p)]
            r = [a - alpha * b for a, b in zip(r, s)]
            u = precondition(r)
            new = total_of([a * b for a, b in zip(r, u)])
            if step + 1 < FIRST_STEPS:
                w = apply(u)
                delta = total_of([a * b for a, b in zip(u, w)])
                beta = new / jnp.maximum(gamma, tiny)
                bend = delta - beta * new / jnp.maximum(alpha, tiny)
                bend = jnp.maximum(bend, jnp.maximum(1e-3 * delta, tiny))
                alpha = new / bend
                p = [a + beta * b for a, b in zip(u, p)]
                s = [a + beta * b for a, b in zip(w, s)]
            gamma = new
        return tuple(x), tuple(r), tuple(u), gamma

    def going(rz):
        return jnp.max((rz > goal).astype(jnp.int32)) > 0

    def body(carry):
        count, _, state = carry
        state = advance(state, STEPS_PER_CHECK)
        return count + 1, going(state[3]), state

    state = opening(zero, target, first_z, first_rz)
    final = lax.while_loop(
        lambda c: jnp.logical_and(c[1], c[0] < MAX_CHECKS),
        body,
        (jnp.int32(0), going(state[3]), state),
    )[2][0]
    chosen = final[0]
    for e in range(1, epochs):
        chosen = jnp.where(tm == e, final[e], chosen)
    out_ref[...] = chosen


def shards(
    ray_basis, delays, ray_station, ray_count, station_var, decay_factor, mode_variance, prior_mean
):
    tm_size = lax.axis_size("tm")
    sta_size = lax.axis_size("sta")
    width = ray_basis.shape[2]
    half = width // 2
    rows = shard_rows(half, sta_size)
    chips = sta_size // CORES
    vmem = pl.BlockSpec(memory_space=pltpu.VMEM)
    hbm = pl.BlockSpec(memory_space=pltpu.HBM)
    dma = pltpu.SemaphoreType.DMA
    packed, variance, prior = pl.pallas_call(
        functools.partial(exchange, tm_size, sta_size, rows, half),
        out_shape=(
            jax.ShapeDtypeStruct((tm_size, sta_size, rows, half), jnp.float32),
            jax.ShapeDtypeStruct((1, width), jnp.float32),
            jax.ShapeDtypeStruct((1, width), jnp.float32),
        ),
        in_specs=[hbm, hbm, hbm, vmem, hbm, hbm, hbm, hbm],
        out_specs=(vmem, vmem, vmem),
        scratch_shapes=[
            pltpu.VMEM(ray_basis.shape, ray_basis.dtype),
            pltpu.VMEM(delays.shape, delays.dtype),
            pltpu.VMEM(ray_station.shape, ray_station.dtype),
            pltpu.SMEM(station_var.shape, station_var.dtype),
            pltpu.VMEM(decay_factor.shape, decay_factor.dtype),
            dma((7,)),
            pltpu.VMEM((sta_size, rows, half), jnp.float32),
            pltpu.VMEM((sta_size, rows, half), jnp.float32),
            dma((sta_size - 1,)),
            dma((sta_size,)),
            dma((tm_size - 1,)),
            dma((tm_size, chips - 1)),
            dma((tm_size, chips)),
            dma((tm_size, sta_size)),
            pltpu.SemaphoreType.REGULAR((2,)),
        ],
        compiler_params=pltpu.CompilerParams(
            collective_id=0, has_side_effects=True, vmem_limit_bytes=VMEM_BYTES
        ),
        name="exchange",
    )(*[
        pltpu.with_memory_space_constraint(x, pltpu.HBM)
        for x in (ray_basis, delays, ray_station)
    ], ray_count, *[
        pltpu.with_memory_space_constraint(x, pltpu.HBM) for x in (
            station_var, decay_factor,
            mode_variance.reshape(1, width), prior_mean.reshape(1, width),
        )
    ])
    packed = packed.reshape(tm_size, sta_size * rows, half)
    return pl.pallas_call(
        functools.partial(solve, tm_size, half),
        out_shape=jax.ShapeDtypeStruct((1, width), jnp.float32),
        in_specs=[vmem, vmem, vmem],
        out_specs=vmem,
        scratch_shapes=[
            pltpu.VMEM((tm_size, 2 * width, width), jnp.bfloat16),
        ],
        compiler_params=pltpu.CompilerParams(vmem_limit_bytes=VMEM_BYTES),
        name="solve",
    )(packed, variance, prior)


def solution(mesh):
    placed = (
        P("tm", "sta", None),
        P("tm", "sta"),
        P("tm", "sta"),
        P("tm", "sta"),
        P("sta"),
        P("tm", None),
        P(),
        P(),
    )
    return jax.shard_map(
        shards, mesh=mesh, in_specs=placed, out_specs=P("tm", None), check_vma=False
    )
```

```python
import functools

import jax
import jax.numpy as jnp
from jax import lax
from jax.experimental import pallas as pl
from jax.experimental.pallas import tpu as pltpu
from jax.sharding import PartitionSpec as P

MESH = pl.DeviceIdType.MESH
CORES = 2
TOL = 2e-8
FIRST_STEPS = 7
STEPS_PER_CHECK = 3
MAX_CHECKS = 700
VMEM_BYTES = 24 << 20


def loop(n, body):
    if n <= 16:
        for i in range(n):
            body(i)
    else:
        def step(i, carry):
            body(i)
            return carry

        lax.fori_loop(0, n, step, 0)


def shard_rows(half, shards):
    rows = 2 * half + 5
    return -(-rows // (8 * shards)) * 8


def exchange(
    tm_size, sta_size, rows, half,
    basis_hbm, delay_hbm, station_hbm, count_ref, var_hbm, decay_hbm, variance_hbm, prior_hbm,
    out_ref, variance_ref, prior_ref,
    basis_ref, delay_ref, station_ref, var_ref, decay_ref, load_sem,
    part, landed, rs_send, rs_recv, z_send, plane_send, core_send, gather_recv, chain,
):
    tm = lax.axis_index("tm")
    sta = lax.axis_index("sta")
    core = sta % CORES
    chip = sta // CORES
    chips = sta_size // CORES

    barrier = pltpu.get_barrier_semaphore()

    def greet_plane(i):
        peer = (sta + 1 + i) % sta_size
        pl.semaphore_signal(barrier, inc=1, device_id=(tm, peer), device_id_type=MESH)

    has_below, has_above = tm > 0, tm < tm_size - 1

    def to_neighbours(below_sem, above_sem):
        @pl.when(has_below)
        def _():
            pl.semaphore_signal(
                below_sem, inc=1, device_id=(tm - 1, sta), device_id_type=MESH
            )

        @pl.when(has_above)
        def _():
            pl.semaphore_signal(
                above_sem, inc=1, device_id=(tm + 1, sta), device_id_type=MESH
            )

    to_neighbours(barrier, barrier)
    loop(sta_size - 1, greet_plane)

    loads = [
        pltpu.make_async_copy(source, target, load_sem.at[i])
        for i, (source, target) in enumerate(
            (
                (var_hbm, var_ref), (station_hbm, station_ref),
                (basis_hbm, basis_ref), (delay_hbm, delay_ref), (decay_hbm, decay_ref),
                (variance_hbm, variance_ref), (prior_hbm, prior_ref),
            )
        )
    ]
    for load in loads:
        load.start()
    for load in loads:
        load.wait()

    rays = basis_ref.shape[1]
    width = 2 * half
    groups = rays // 128
    local = station_ref[...] - sta * var_ref.shape[0]
    slots = lax.broadcasted_iota(jnp.int32, (1, rays), 1)
    noise = jnp.ones((1, rays), jnp.float32)
    for s in range(var_ref.shape[0]):
        noise = jnp.where(local == s, var_ref[s], noise)
    weight = jnp.where(slots < count_ref[...], 1.0 / noise, 0.0)
    square = jnp.concatenate(
        [weight[:, g * 128 : (g + 1) * 128] for g in range(groups)]
        + [jnp.zeros((128 - groups, 128), jnp.float32)],
        axis=0,
    )
    columns = square.T
    weighted = jnp.concatenate(
        [
            (basis_ref[0, g * 128 : (g + 1) * 128, :].astype(jnp.float32) * columns[:, g : g + 1])
            for g in range(groups)
        ],
        axis=0,
    ).astype(jnp.bfloat16)
    basis = basis_ref[0]
    outer = (((0,), (0,)), ((), ()))
    left = lax.dot_general(
        weighted, basis[:, :half], outer, preferred_element_type=jnp.float32
    )
    corner = lax.dot_general(
        weighted[:, half:], basis[:, half:], outer, preferred_element_type=jnp.float32
    )
    drive = jnp.dot(delay_ref[...], weighted, preferred_element_type=jnp.float32)
    keep = jnp.where(jnp.full((1, width), sta, jnp.int32) == 0, decay_ref[...], 0.0)
    row_id = lax.broadcasted_iota(jnp.int32, (half, half), 0)
    col_id = lax.broadcasted_iota(jnp.int32, (half, half), 1)
    mixed = jnp.where(row_id >= col_id, left[:half], corner)
    tail = [jnp.sum(jnp.where(row_id == col_id, corner, 0.0), axis=0, keepdims=True)]
    tail += [drive[:, i * half : (i + 1) * half] for i in range(2)]
    tail += [keep[:, i * half : (i + 1) * half] for i in range(2)]
    pad = sta_size * rows - 2 * half - 5
    flat = jnp.concatenate(
        [mixed, left[half:]] + tail + [jnp.zeros((pad, half), jnp.float32)], axis=0
    )
    for s in range(sta_size):
        part[s] = flat[s * rows : (s + 1) * rows]

    pl.semaphore_wait(
        barrier, sta_size - 1 + has_below.astype(jnp.int32) + has_above.astype(jnp.int32)
    )

    def scatter(i):
        peer = (sta + 1 + i) % sta_size
        return pltpu.make_async_remote_copy(
            src_ref=part.at[peer], dst_ref=landed.at[sta],
            send_sem=rs_send.at[i], recv_sem=rs_recv.at[sta],
            device_id=(tm, peer), device_id_type=MESH,
        )

    def scattered(i):
        peer = (sta + 1 + i) % sta_size
        return pltpu.make_async_remote_copy(
            src_ref=part.at[peer], dst_ref=landed.at[peer],
            send_sem=rs_send.at[i], recv_sem=rs_recv.at[peer],
            device_id=(tm, peer), device_id_type=MESH,
        )

    loop(sta_size - 1, lambda i: scatter(i).start())

    def widen(i):
        to_neighbours(chain.at[0], chain.at[1])

        @pl.when(has_above)
        def _():
            pl.semaphore_wait(chain.at[0], 1)

        @pl.when(has_below)
        def _():
            pl.semaphore_wait(chain.at[1], 1)

    loop(tm_size - 2, widen)
    loop(sta_size - 1, lambda i: scattered(i).wait_recv())
    total = part[sta]
    if sta_size <= 16:
        for i in range(sta_size - 1):
            total = total + landed[(sta + 1 + i) % sta_size]
    else:
        total = lax.fori_loop(
            0, sta_size - 1, lambda i, t: t + landed[(sta + 1 + i) % sta_size], total
        )
    out_ref[tm, sta] = total

    def slot_copy(z, s, send_sem, device):
        return pltpu.make_async_remote_copy(
            src_ref=out_ref.at[z, s], dst_ref=out_ref.at[z, s],
            send_sem=send_sem, recv_sem=gather_recv.at[z, s],
            device_id=device, device_id_type=MESH,
        )

    def column_copy(i):
        return slot_copy(tm, sta, z_send.at[i], ((tm + 1 + i) % tm_size, sta))

    def plane_copy(z, i):
        peer = ((chip + 1 + i) % chips) * CORES + core
        return slot_copy(z, sta, plane_send.at[z, i], (tm, peer))

    def core_copy(z, c):
        return slot_copy(z, c * CORES + core, core_send.at[z, c], (tm, chip * CORES + 1 - core))

    def spread(z):
        loop(chips - 1, lambda i: plane_copy(z, i).start())
        core_copy(z, chip).start()

    loop(tm_size - 1, lambda i: column_copy(i).start())
    spread(tm)

    def relay(i):
        z = (tm + 1 + i) % tm_size
        slot_copy(z, sta, core_send.at[z, chip], (tm, sta)).wait_recv()
        spread(z)

    loop(tm_size - 1, relay)

    def share(j):
        z = (tm + j) % tm_size

        def one(i):
            c = (chip + 1 + i) % chips
            slot_copy(z, c * CORES + core, core_send.at[z, c], (tm, sta)).wait_recv()
            core_copy(z, c).start()

        loop(chips - 1, one)

    loop(tm_size, share)

    def collect(z):
        def one(c):
            slot_copy(
                z, c * CORES + 1 - core, core_send.at[z, c], (tm, sta)
            ).wait_recv()

        loop(chips, one)

    loop(tm_size, collect)
    loop(sta_size - 1, lambda i: scatter(i).wait_send())
    loop(tm_size - 1, lambda i: column_copy(i).wait_send())

    def drain(z):
        loop(chips - 1, lambda i: plane_copy(z, i).wait_send())
        loop(chips, lambda c: core_copy(z, c).wait_send())

    loop(tm_size, drain)


def total_of(rows):
    acc = rows[0]
    for row in rows[1:]:
        acc = acc + row
    return jnp.sum(acc, axis=1, keepdims=True)


def solve(epochs, half, packed_ref, variance_ref, prior_ref, out_ref, table):
    width = 2 * half
    tm = lax.axis_index("tm")
    row_id = lax.broadcasted_iota(jnp.int32, (half, half), 0)
    col_id = lax.broadcasted_iota(jnp.int32, (half, half), 1)
    diagonal = row_id == col_id
    decay, drive, info_diag = [], [], []
    for e in range(epochs):
        mixed = packed_ref[e, :half]
        lower = packed_ref[e, half : 2 * half]
        tail = packed_ref[e, 2 * half : 2 * half + 8]
        flipped = mixed.T
        upper = jnp.where(row_id >= col_id, mixed, flipped)
        corner = jnp.where(
            row_id < col_id, mixed, jnp.where(diagonal, tail[0:1], flipped)
        )
        matrix = jnp.concatenate(
            [
                jnp.concatenate([upper, lower.T], axis=1),
                jnp.concatenate([lower, corner], axis=1),
            ],
            axis=0,
        )
        high = matrix.astype(jnp.bfloat16)
        table[e, :width] = high
        table[e, width:] = (matrix - high.astype(jnp.float32)).astype(jnp.bfloat16)
        info_diag.append(
            jnp.concatenate(
                [jnp.sum(jnp.where(diagonal, mixed, 0.0), axis=0, keepdims=True), tail[0:1]],
                axis=1,
            )
        )
        drive.append(jnp.concatenate([tail[1:2], tail[2:3]], axis=1))
        decay.append(jnp.concatenate([tail[3:4], tail[4:5]], axis=1))
    variance = variance_ref[...]
    inverse_noise = [1.0 / ((1.0 - d * d) * variance) for d in decay]
    off = [-decay[e] * inverse_noise[e] for e in range(epochs)]
    main = []
    for e in range(epochs):
        value = inverse_noise[e]
        if e + 1 < epochs:
            value = value + decay[e + 1] * decay[e + 1] * inverse_noise[e + 1]
        main.append(value)
    target = list(drive)
    target[0] = target[0] + inverse_noise[0] * (decay[0] * prior_ref[...])

    pivot_inverse, ratio = [], []
    for e in range(epochs):
        pivot = main[e] + info_diag[e]
        if e:
            ratio.append(off[e] * pivot_inverse[-1])
            pivot = pivot - ratio[-1] * off[e]
        pivot_inverse.append(1.0 / pivot)

    def eliminate(r):
        y = [r[0]]
        for e in range(1, epochs):
            y.append(r[e] - ratio[e - 1] * y[-1])
        z = [None] * epochs
        z[-1] = y[-1] * pivot_inverse[-1]
        for e in range(epochs - 2, -1, -1):
            z[e] = y[e] * pivot_inverse[e] - ratio[e] * z[e + 1]
        return z

    if epochs <= 8:
        ones = jnp.ones((1, width), jnp.float32)
        units = [
            eliminate([ones if e == f else jnp.zeros_like(ones) for e in range(epochs)])
            for f in range(epochs)
        ]

    def precondition(r):
        if epochs > 8:
            return eliminate(r)
        z = []
        for e in range(epochs):
            terms = [units[f][e] * r[f] for f in range(epochs)]
            while len(terms) > 1:
                terms = [sum(terms[i : i + 2][1:], terms[i]) for i in range(0, len(terms), 2)]
            z.append(terms[0])
        return z

    pick = lax.broadcasted_iota(jnp.int32, (8, width), 0)

    def apply(p):
        result = []
        for e in range(epochs):
            first = p[e].astype(jnp.bfloat16).astype(jnp.float32)
            rest = p[e] - first
            second = rest.astype(jnp.bfloat16).astype(jnp.float32)
            third = rest - second
            stacked = jnp.where(
                pick == 0, first, jnp.where(pick == 1, second, jnp.where(pick == 2, third, 0.0))
            ).astype(jnp.bfloat16)
            both = jnp.concatenate([stacked, stacked], axis=1)
            product = jnp.dot(both, table[e], preferred_element_type=jnp.float32)
            value = main[e] * p[e] + jnp.sum(product, axis=0, keepdims=True)
            if e:
                value = value + off[e] * p[e - 1]
            if e + 1 < epochs:
                value = value + off[e + 1] * p[e + 1]
            result.append(value)
        return result

    tiny = 1e-30
    zero = [jnp.zeros((1, width), jnp.float32)] * epochs
    first_z = precondition(target)
    first_rz = total_of([a * b for a, b in zip(target, first_z)])
    goal = TOL * first_rz

    def advance(state, steps):
        x, r, p, rz = list(state[0]), list(state[1]), list(state[2]), state[3]
        for _ in range(steps):
            q = apply(p)
            bend = total_of([a * b for a, b in zip(p, q)])
            alpha = rz / jnp.maximum(bend, tiny)
            x = [a + alpha * b for a, b in zip(x, p)]
            r = [a - alpha * b for a, b in zip(r, q)]
            z = precondition(r)
            new = total_of([a * b for a, b in zip(r, z)])
            beta = new / jnp.maximum(rz, tiny)
            p = [a + beta * b for a, b in zip(z, p)]
            rz = new
        return tuple(x), tuple(r), tuple(p), rz

    def opening(x, r, u, gamma):
        w = apply(u)
        alpha = gamma / jnp.maximum(total_of([a * b for a, b in zip(u, w)]), tiny)
        p, s = u, w
        for step in range(FIRST_STEPS):
            x = [a + alpha * b for a, b in zip(x, p)]
            r = [a - alpha * b for a, b in zip(r, s)]
            u = precondition(r)
            new = total_of([a * b for a, b in zip(r, u)])
            if step + 1 < FIRST_STEPS:
                w = apply(u)
                delta = total_of([a * b for a, b in zip(u, w)])
                beta = new / jnp.maximum(gamma, tiny)
                bend = delta - beta * new / jnp.maximum(alpha, tiny)
                bend = jnp.maximum(bend, jnp.maximum(1e-3 * delta, tiny))
                alpha = new / bend
                p = [a + beta * b for a, b in zip(u, p)]
                s = [a + beta * b for a, b in zip(w, s)]
            gamma = new
        return tuple(x), tuple(r), tuple(u), gamma

    def going(rz):
        return jnp.max((rz > goal).astype(jnp.int32)) > 0

    def body(carry):
        count, _, state = carry
        state = advance(state, STEPS_PER_CHECK)
        return count + 1, going(state[3]), state

    state = opening(zero, target, first_z, first_rz)
    final = lax.while_loop(
        lambda c: jnp.logical_and(c[1], c[0] < MAX_CHECKS),
        body,
        (jnp.int32(0), going(state[3]), state),
    )[2][0]
    chosen = final[0]
    for e in range(1, epochs):
        chosen = jnp.where(tm == e, final[e], chosen)
    out_ref[...] = chosen


def shards(
    ray_basis, delays, ray_station, ray_count, station_var, decay_factor, mode_variance, prior_mean
):
    tm_size = lax.axis_size("tm")
    sta_size = lax.axis_size("sta")
    width = ray_basis.shape[2]
    half = width // 2
    rows = shard_rows(half, sta_size)
    chips = sta_size // CORES
    vmem = pl.BlockSpec(memory_space=pltpu.VMEM)
    hbm = pl.BlockSpec(memory_space=pltpu.HBM)
    dma = pltpu.SemaphoreType.DMA
    packed, variance, prior = pl.pallas_call(
        functools.partial(exchange, tm_size, sta_size, rows, half),
        out_shape=(
            jax.ShapeDtypeStruct((tm_size, sta_size, rows, half), jnp.float32),
            jax.ShapeDtypeStruct((1, width), jnp.float32),
            jax.ShapeDtypeStruct((1, width), jnp.float32),
        ),
        in_specs=[hbm, hbm, hbm, vmem, hbm, hbm, hbm, hbm],
        out_specs=(vmem, vmem, vmem),
        scratch_shapes=[
            pltpu.VMEM(ray_basis.shape, ray_basis.dtype),
            pltpu.VMEM(delays.shape, delays.dtype),
            pltpu.VMEM(ray_station.shape, ray_station.dtype),
            pltpu.SMEM(station_var.shape, station_var.dtype),
            pltpu.VMEM(decay_factor.shape, decay_factor.dtype),
            dma((7,)),
            pltpu.VMEM((sta_size, rows, half), jnp.float32),
            pltpu.VMEM((sta_size, rows, half), jnp.float32),
            dma((sta_size - 1,)),
            dma((sta_size,)),
            dma((tm_size - 1,)),
            dma((tm_size, chips - 1)),
            dma((tm_size, chips)),
            dma((tm_size, sta_size)),
            pltpu.SemaphoreType.REGULAR((2,)),
        ],
        compiler_params=pltpu.CompilerParams(
            collective_id=0, has_side_effects=True, vmem_limit_bytes=VMEM_BYTES
        ),
        name="exchange",
    )(*[
        pltpu.with_memory_space_constraint(x, pltpu.HBM)
        for x in (ray_basis, delays, ray_station)
    ], ray_count, *[
        pltpu.with_memory_space_constraint(x, pltpu.HBM) for x in (
            station_var, decay_factor,
            mode_variance.reshape(1, width), prior_mean.reshape(1, width),
        )
    ])
    packed = packed.reshape(tm_size, sta_size * rows, half)
    return pl.pallas_call(
        functools.partial(solve, tm_size, half),
        out_shape=jax.ShapeDtypeStruct((1, width), jnp.float32),
        in_specs=[vmem, vmem, vmem],
        out_specs=vmem,
        scratch_shapes=[
            pltpu.VMEM((tm_size, 2 * width, width), jnp.bfloat16),
        ],
        compiler_params=pltpu.CompilerParams(vmem_limit_bytes=VMEM_BYTES),
        name="solve",
    )(packed, variance, prior)


def solution(mesh):
    placed = (
        P("tm", "sta", None),
        P("tm", "sta"),
        P("tm", "sta"),
        P("tm", "sta"),
        P("sta"),
        P("tm", None),
        P(),
        P(),
    )
    return jax.shard_map(
        shards, mesh=mesh, in_specs=placed, out_specs=P("tm", None), check_vma=False
    )
```
